32 devices in a mesh: box: 4 (over y, core), dir: 8 (over z, x).
Axes of the slice: x: 2, y: 2, z: 4, core: 2. Of those that a mesh axis runs over, the one named last changes fastest.
Arguments:
- currents: bfloat16 [256, 2, 256, 128], P(('box', 'dir')), may hold values from -6 to 6
- near_blocks: bfloat16 [256, 3, 2, 256, 256], P(('box', 'dir')), may hold values from -0.21875 to 0.21875
- near_mask: int32 [2, 256], replicated, may hold values 0 or 1
- aggregate: bfloat16 [2, 512, 256], replicated, may hold values from -0.375 to 0.375
- disaggregate: bfloat16 [2, 256, 512], replicated, may hold values from -0.25 to 0.25
- centers: float32 [3, 256], replicated, may hold values from 0 to 16
Outputs:
- fields: bfloat16 [256, 2, 256, 128], P(('box', 'dir'))
The draws below stay inside these ranges and needn't reach their ends.
All inputs are finite; a program needn't handle non-finite values.
Results may differ from the reference program's by a relative error of at most 0.0054.
Values may be sent and summed in bfloat16 or wider, within the bound.
No kernel may reach another device: no remote copies, remote signals or barrier semaphores. Data moves between devices by JAX's collectives and lax.ppermute only.
A program may use at most 64 MiB of HBM per device.

```python
import math
import jax
import jax.numpy as jnp
from jax import lax

NU = 256
K = 512
A = 128
BOXES = 256


def plant(values, rng, smallest, largest):
    extent = values.shape
    spot = [jax.random.randint(jax.random.fold_in(rng, axis), (), 0, extent[axis]) for axis in range(len(extent))]
    values = values.at[tuple(spot)].set(smallest)
    longest = extent.index(max(extent))
    spot[longest] = (spot[longest] + 1) % extent[longest]
    return values.at[tuple(spot)].set(largest)


def shard_levels(key, shape, split, least, largest):
    def one(position, shards_of):
        draws = jax.random.uniform(jax.random.fold_in(jax.random.fold_in(key, 6), position), (shards_of,), jnp.float32, least / len(split), largest / len(split))
        return jnp.repeat(jnp.exp(draws), shape[position] // shards_of).reshape((-1,) + (1,) * (len(shape) - position - 1))

    factor_of = one(*split[0])
    for cut in split[1:]:
        factor_of = factor_of * one(*cut)
    return factor_of


def centred(own_key, dims, scale, limit, pieces=(), held_as=jnp.bfloat16):
    entries = jax.random.normal(own_key, dims, jnp.float32) * scale
    if len(pieces) > 0:
        entries = shard_levels(own_key, dims, pieces, -0.22, 0.18) * entries
    return jnp.clip(entries, min=-limit, max=limit).astype(held_as)


def setup_inputs(seed: int = 0) -> dict:
    key_list = jax.random.split(jax.random.key(seed), 7)
    currents = centred(key_list[0], (BOXES, 2, NU, A), 1.0, 6.0, ((0, 32),))
    near_blocks = centred(key_list[1], (BOXES, 3, 2, NU, NU), (3 * NU) ** -0.5, 0.21875, ((0, 32),))
    near_mask = plant((jax.random.randint(key_list[2], (2, BOXES), 0, 4) < 3).astype(jnp.int32), jax.random.fold_in(key_list[2], 1), 0, 1)
    aggregate = centred(key_list[3], (2, K, NU), NU ** -0.5, 0.375)
    disaggregate = centred(key_list[4], (2, NU, K), K ** -0.5, 0.25)
    centers = jnp.clip(jax.random.uniform(key_list[5], (3, BOXES), jnp.float32, 0.0, 16.0), 0.0, 16.0)
    return {"currents": currents, "near_blocks": near_blocks, "near_mask": near_mask, "aggregate": aggregate, "disaggregate": disaggregate, "centers": centers}


wave_number = 2.0
far_gain = 8.0
golden_turn = 2.399963229728653

def direction_cosines(count, first, many):
    order = (first + jnp.arange(many, dtype=jnp.int32)).astype(jnp.float32)
    height = 1.0 - (2.0 * order + 1.0) / count
    radial = jnp.sqrt(1.0 - height * height)
    azimuth = order * golden_turn
    return (radial * jnp.cos(azimuth), radial * jnp.sin(azimuth), height)

def phase_angles(points, first, many, count):
    dir_x, dir_y, dir_z = direction_cosines(count, first, many)
    return wave_number * (points[0][:, None] * dir_x[None, :] + points[1][:, None] * dir_y[None, :] + points[2][:, None] * dir_z[None, :])

def far_matrix(centers, near_mask):
    total_boxes = centers.shape[1]
    squared = jnp.zeros((total_boxes, total_boxes), jnp.float32)
    for axis_number in range(3):
        spread = centers[axis_number][:, None] - centers[axis_number][None, :]
        squared = squared + spread * spread
    spacing = jnp.sqrt(1.0 + squared)
    kernel = jnp.cos(wave_number * spacing) / (1.0 + spacing) * (far_gain / math.sqrt(total_boxes))
    rows = jnp.arange(total_boxes, dtype=jnp.int32)[:, None]
    cols = jnp.arange(total_boxes, dtype=jnp.int32)[None, :]
    linked = (cols == rows) | (cols == rows - 1) & (near_mask[0][:, None] == 1) | (cols == rows + 1) & (near_mask[1][:, None] == 1)
    return jnp.where(linked, 0.0, kernel).astype(jnp.bfloat16)

def reference(currents, near_blocks, near_mask, aggregate, disaggregate, centers):
    flt = jnp.float32
    total_boxes = centers.shape[1]
    padded = jnp.pad(currents.astype(flt), ((1, 1), (0, 0), (0, 0), (0, 0)))
    left_mask = near_mask[0].astype(flt)
    right_mask = near_mask[1].astype(flt)
    block = math.gcd(total_boxes, 64)

    def near_part(number):
        first_box = number * block
        blocks = lax.dynamic_slice_in_dim(near_blocks, first_box, block, 0).astype(flt)
        window = lax.dynamic_slice_in_dim(padded, first_box, block + 2, 0)
        left_on = lax.dynamic_slice_in_dim(left_mask, first_box, block, 0)[:, None, None, None]
        right_on = lax.dynamic_slice_in_dim(right_mask, first_box, block, 0)[:, None, None, None]
        stacked = jnp.stack([window[1:-1], window[:-2] * left_on, window[2:] * right_on], 1)

        def product(left, right):
            return jnp.einsum('bjuv,bjva->bua', left, right, precision=lax.Precision.HIGHEST)
        near_re = product(blocks[:, :, 0], stacked[:, :, 0]) - product(blocks[:, :, 1], stacked[:, :, 1])
        near_im = product(blocks[:, :, 0], stacked[:, :, 1]) + product(blocks[:, :, 1], stacked[:, :, 0])
        return jnp.stack([near_re, near_im], 1)
    near = lax.map(near_part, jnp.arange(total_boxes // block, dtype=jnp.int32)).reshape(currents.shape)
    translate = far_matrix(centers, near_mask).astype(flt)
    cur_re = currents[:, 0].astype(flt)
    cur_im = currents[:, 1].astype(flt)
    width = math.gcd(K, 32)

    def far_step(carry, number):
        first_dir = number * width
        agg_part = lax.dynamic_slice_in_dim(aggregate, first_dir, width, 1).astype(flt)
        dis_part = lax.dynamic_slice_in_dim(disaggregate, first_dir, width, 2).astype(flt)

        def gather_in(matrix, vectors):
            return jnp.einsum('ku,bua->bka', matrix, vectors, precision=lax.Precision.HIGHEST)
        pat_re = gather_in(agg_part[0], cur_re) - gather_in(agg_part[1], cur_im)
        pat_im = gather_in(agg_part[0], cur_im) + gather_in(agg_part[1], cur_re)
        theta = phase_angles(centers, first_dir, width, K)
        cosine = jnp.cos(theta)[:, :, None]
        sine = jnp.sin(theta)[:, :, None]
        pattern = jnp.stack([cosine * pat_re + sine * pat_im, cosine * pat_im - sine * pat_re], 2).astype(jnp.bfloat16).astype(flt)
        summed = jnp.dot(translate, pattern.reshape(total_boxes, -1), precision=lax.Precision.HIGHEST).reshape(pattern.shape)
        sum_re = summed[:, :, 0]
        sum_im = summed[:, :, 1]
        received = jnp.stack([cosine * sum_re - sine * sum_im, cosine * sum_im + sine * sum_re], 2).astype(jnp.bfloat16).astype(flt)

        def spread_out(matrix, vectors):
            return jnp.einsum('uk,bka->bua', matrix, vectors, precision=lax.Precision.HIGHEST)
        far_re = spread_out(dis_part[0], received[:, :, 0]) - spread_out(dis_part[1], received[:, :, 1])
        far_im = spread_out(dis_part[0], received[:, :, 1]) + spread_out(dis_part[1], received[:, :, 0])
        return (carry + jnp.stack([far_re, far_im], 1), None)
    far, unused = lax.scan(far_step, jnp.zeros(currents.shape, flt), jnp.arange(K // width, dtype=jnp.int32))
    return (near + far).astype(jnp.bfloat16)
```

```python
import functools
import math

import jax
import jax.numpy as jnp
from jax import lax
from jax.experimental import pallas as pl
from jax.experimental.pallas import tpu as pltpu
from jax.sharding import PartitionSpec as P

wave_number = 2.0
far_gain = 8.0
golden_turn = 2.399963229728653
axes = ("box", "dir")
chunks_wanted = 1


def direction_cosines(count):
    order = jnp.arange(count, dtype=jnp.int32).astype(jnp.float32)
    height = 1.0 - (2.0 * order + 1.0) / count
    radial = jnp.sqrt(1.0 - height * height)
    azimuth = order * golden_turn
    return (radial * jnp.cos(azimuth), radial * jnp.sin(azimuth), height)


def phase_angles(points, count):
    dir_x, dir_y, dir_z = direction_cosines(count)
    return wave_number * (
        points[0][:, None] * dir_x[None, :]
        + points[1][:, None] * dir_y[None, :]
        + points[2][:, None] * dir_z[None, :]
    )


def far_matrix(centers, near_mask):
    total_boxes = centers.shape[1]
    squared = jnp.zeros((total_boxes, total_boxes), jnp.float32)
    for axis_number in range(3):
        spread = centers[axis_number][:, None] - centers[axis_number][None, :]
        squared = squared + spread * spread
    spacing = jnp.sqrt(1.0 + squared)
    kernel = jnp.cos(wave_number * spacing) / (1.0 + spacing) * (far_gain / math.sqrt(total_boxes))
    rows = jnp.arange(total_boxes, dtype=jnp.int32)[:, None]
    cols = jnp.arange(total_boxes, dtype=jnp.int32)[None, :]
    linked = (
        (cols == rows)
        | (cols == rows - 1) & (near_mask[0][:, None] == 1)
        | (cols == rows + 1) & (near_mask[1][:, None] == 1)
    )
    return jnp.where(linked, 0.0, kernel).astype(jnp.bfloat16)


def swap_matrix(outer, inner):
    size = outer * inner
    row = lax.broadcasted_iota(jnp.int32, (size, size), 0)
    col = lax.broadcasted_iota(jnp.int32, (size, size), 1)
    return ((row % inner) * outer + row // inner == col).astype(jnp.bfloat16)


def pack_body(currents_ref, swap_ref, *refs, devices, angles_each, group):
    outs, turned_ref = refs[:-1], refs[-1]
    boxes, _, unknowns, angles = currents_ref.shape
    rows = 2 * boxes
    for part in range(2):
        for box in range(boxes):
            turned_ref[part * boxes + box] = currents_ref[box, part].T
    per_out = angles_each // len(outs)
    for first in range(0, angles, group):
        own, device = divmod(first, devices)
        tile = turned_ref[:, first : first + group, :].reshape(rows * group, unknowns)
        mixed = jnp.dot(swap_ref[...], tile, preferred_element_type=jnp.float32)
        which, slot = divmod(own, per_out)
        outs[which][device : device + group, slot] = mixed.astype(jnp.bfloat16).reshape(
            group, rows, unknowns
        )


def pack(currents, devices, chunks):
    boxes, _, unknowns, angles = currents.shape
    angles_each = angles // devices
    group = math.gcd(16, devices)
    rows = 2 * boxes
    body = functools.partial(pack_body, devices=devices, angles_each=angles_each, group=group)
    shape = jax.ShapeDtypeStruct((devices, angles_each // chunks, rows, unknowns), jnp.bfloat16)
    return pl.pallas_call(
        body,
        out_shape=[shape] * chunks,
        scratch_shapes=[pltpu.VMEM((rows, angles, unknowns), jnp.bfloat16)],
        name="pack",
    )(currents, swap_matrix(group, rows))


def unpack_body(near_ref, swap_ref, *refs, devices, angles_each, group):
    ins, out_ref, turned_ref = refs[:-2], refs[-2], refs[-1]
    boxes, _, unknowns, angles = out_ref.shape
    rows = 2 * boxes
    per_in = angles_each // len(ins)
    for first in range(0, angles, group):
        own, device = divmod(first, devices)
        which, slot = divmod(own, per_in)
        tile = ins[which][device : device + group, slot].reshape(rows * group, unknowns)
        mixed = jnp.dot(swap_ref[...], tile, preferred_element_type=jnp.float32)
        turned_ref[:, first : first + group, :] = mixed.astype(jnp.bfloat16).reshape(
            rows, group, unknowns
        )
    for part in range(2):
        for box in range(boxes):
            far = turned_ref[part * boxes + box].T.astype(jnp.float32)
            out_ref[box, part] = (near_ref[box, part] + far).astype(jnp.bfloat16)


def unpack(near, pieces, devices):
    boxes, _, unknowns, angles = near.shape
    angles_each = angles // devices
    group = math.gcd(16, devices)
    rows = 2 * boxes
    body = functools.partial(unpack_body, devices=devices, angles_each=angles_each, group=group)
    return pl.pallas_call(
        body,
        out_shape=jax.ShapeDtypeStruct(near.shape, jnp.bfloat16),
        scratch_shapes=[pltpu.VMEM((rows, angles, unknowns), jnp.bfloat16)],
        name="unpack",
    )(near, swap_matrix(rows, group), *pieces)


def far_body(arrived_ref, gather_ref, spread_ref, translate_ref, cos_ref, sin_ref, out_ref, sum_ref):
    devices, _, rows, unknowns = arrived_ref.shape
    boxes = rows // 2
    total = devices * boxes
    width = cos_ref.shape[1]
    block = pl.program_id(1)
    arrived = arrived_ref[:, 0].reshape(devices * rows, unknowns)
    by_re = jnp.dot(arrived, gather_ref[0], preferred_element_type=jnp.float32)
    by_im = jnp.dot(arrived, gather_ref[1], preferred_element_type=jnp.float32)
    by_re = by_re.reshape(devices, 2, boxes, width)
    by_im = by_im.reshape(devices, 2, boxes, width)
    pat_re = (by_re[:, 0] - by_im[:, 1]).reshape(total, width)
    pat_im = (by_re[:, 1] + by_im[:, 0]).reshape(total, width)
    cosine = cos_ref[...]
    sine = sin_ref[...]
    out_re = (cosine * pat_re + sine * pat_im).astype(jnp.bfloat16)
    out_im = (cosine * pat_im - sine * pat_re).astype(jnp.bfloat16)
    translate = translate_ref[...]
    sum_re = jnp.dot(translate, out_re, preferred_element_type=jnp.float32)
    sum_im = jnp.dot(translate, out_im, preferred_element_type=jnp.float32)
    rec_re = (cosine * sum_re - sine * sum_im).astype(jnp.bfloat16)
    rec_im = (cosine * sum_im + sine * sum_re).astype(jnp.bfloat16)
    far = jnp.dot(rec_re, spread_ref[0], preferred_element_type=jnp.float32) + jnp.dot(
        rec_im, spread_ref[1], preferred_element_type=jnp.float32
    )

    @pl.when(block == 0)
    def _():
        sum_ref[...] = far

    @pl.when(block != 0)
    def _():
        sum_ref[...] += far

    @pl.when(block == pl.num_programs(1) - 1)
    def _():
        whole = sum_ref[...]
        real = whole[:, :unknowns].reshape(devices, 1, boxes, unknowns)
        imag = whole[:, unknowns:].reshape(devices, 1, boxes, unknowns)
        both = jnp.concatenate([real, imag], 1).reshape(devices, rows, unknowns)
        out_ref[:, 0] = both.astype(jnp.bfloat16)


def far_field(arrived, gather, spread, translate, cosine, sine):
    devices, slots, rows, unknowns = arrived.shape
    total, count = cosine.shape
    width = math.gcd(count, 256)
    return pl.pallas_call(
        far_body,
        grid=(slots, count // width),
        in_specs=[
            pl.BlockSpec((devices, 1, rows, unknowns), lambda i, j: (0, i, 0, 0)),
            pl.BlockSpec((2, unknowns, width), lambda i, j: (0, 0, j)),
            pl.BlockSpec((2, width, 2 * unknowns), lambda i, j: (0, j, 0)),
            pl.BlockSpec((total, total), lambda i, j: (0, 0)),
            pl.BlockSpec((total, width), lambda i, j: (0, j)),
            pl.BlockSpec((total, width), lambda i, j: (0, j)),
        ],
        out_specs=pl.BlockSpec((devices, 1, rows, unknowns), lambda i, j: (0, i, 0, 0)),
        out_shape=jax.ShapeDtypeStruct(arrived.shape, jnp.bfloat16),
        scratch_shapes=[pltpu.VMEM((total, 2 * unknowns), jnp.float32)],
        name="far",
    )(arrived, gather, spread, translate, cosine, sine)


def near_body(place_ref, mask_ref, currents_ref, low_ref, high_ref, blocks_ref, out_ref):
    boxes, _, unknowns, angles = currents_ref.shape
    box = pl.program_id(0)
    own = place_ref[0] * boxes + box

    def both(block):
        return jnp.concatenate([block[0], block[1]], 1)

    zero = jnp.zeros((unknowns, 2 * angles), jnp.bfloat16)
    here = both(currents_ref[box])
    before = jnp.where(box == 0, both(low_ref[0]), both(currents_ref[jnp.maximum(box - 1, 0)]))
    after = jnp.where(
        box == boxes - 1, both(high_ref[0]), both(currents_ref[jnp.minimum(box + 1, boxes - 1)])
    )
    before = jnp.where(mask_ref[0, own] == 1, before, zero)
    after = jnp.where(mask_ref[1, own] == 1, after, zero)
    by_re = jnp.zeros((unknowns, 2 * angles), jnp.float32)
    by_im = jnp.zeros((unknowns, 2 * angles), jnp.float32)
    for which, vectors in enumerate((here, before, after)):
        by_re += jnp.dot(blocks_ref[0, which, 0], vectors, preferred_element_type=jnp.float32)
        by_im += jnp.dot(blocks_ref[0, which, 1], vectors, preferred_element_type=jnp.float32)
    out_ref[0, 0] = by_re[:, :angles] - by_im[:, angles:]
    out_ref[0, 1] = by_re[:, angles:] + by_im[:, :angles]


def near_field(currents, low, high, near_blocks, near_mask, place):
    boxes, _, unknowns, angles = currents.shape
    whole = pl.BlockSpec(currents.shape, lambda i, *_: (0, 0, 0, 0))
    edge = pl.BlockSpec(low.shape, lambda i, *_: (0, 0, 0, 0))
    return pl.pallas_call(
        near_body,
        grid_spec=pltpu.PrefetchScalarGridSpec(
            num_scalar_prefetch=2,
            grid=(boxes,),
            in_specs=[
                whole,
                edge,
                edge,
                pl.BlockSpec((1, 3, 2, unknowns, unknowns), lambda i, *_: (i, 0, 0, 0, 0)),
            ],
            out_specs=pl.BlockSpec((1, 2, unknowns, angles), lambda i, *_: (i, 0, 0, 0)),
        ),
        out_shape=jax.ShapeDtypeStruct(currents.shape, jnp.float32),
        name="near",
    )(place, near_mask, currents, low, high, near_blocks)


def edges(currents):
    count = lax.axis_size(axes)
    forward = [(i, i + 1) for i in range(count - 1)]
    backward = [(i + 1, i) for i in range(count - 1)]
    low = lax.ppermute(currents[-1:], axes, forward)
    high = lax.ppermute(currents[:1], axes, backward)
    return low, high


def local(currents, near_blocks, near_mask, aggregate, disaggregate, centers):
    devices = lax.axis_size(axes)
    angles_each = currents.shape[3] // devices
    chunks = math.gcd(chunks_wanted, angles_each)
    dir_count = aggregate.shape[1]
    place = lax.axis_index(axes).astype(jnp.int32).reshape(1)

    packed = pack(currents, devices, chunks)
    arrived = [lax.all_to_all(x, axes, split_axis=0, concat_axis=0, tiled=True) for x in packed]
    low, high = edges(currents)
    gather = aggregate.transpose(0, 2, 1)
    turned = disaggregate.transpose(0, 2, 1)
    spread = jnp.stack(
        [
            jnp.concatenate([turned[0], turned[1]], 1),
            jnp.concatenate([-turned[1], turned[0]], 1),
        ]
    )
    translate = far_matrix(centers, near_mask)
    theta = phase_angles(centers, dir_count)
    cosine = jnp.cos(theta)
    sine = jnp.sin(theta)
    far = [far_field(x, gather, spread, translate, cosine, sine) for x in arrived]
    pieces = [lax.all_to_all(x, axes, split_axis=0, concat_axis=0, tiled=True) for x in far]
    near = near_field(currents, low, high, near_blocks, near_mask, place)
    return unpack(near, pieces, devices)


def solution(mesh):
    return jax.shard_map(
        local,
        mesh=mesh,
        in_specs=(
            P(axes, None, None, None),
            P(axes, None, None, None, None),
            P(),
            P(),
            P(),
            P(),
        ),
        out_specs=P(axes, None, None, None),
        check_vma=False,
    )
```

```python
import functools
import math

import jax
import jax.numpy as jnp
from jax import lax
from jax.experimental import pallas as pl
from jax.experimental.pallas import tpu as pltpu
from jax.sharding import PartitionSpec as P


wave_number = 2.0
far_gain = 8.0
golden_turn = 2.399963229728653
axes = ("box", "dir")
chunks_wanted = 1
far_rows = 512
far_slots = 1
hbm = pl.BlockSpec(memory_space=pltpu.HBM)
vmem = pl.BlockSpec(memory_space=pltpu.VMEM)
params = pltpu.CompilerParams(vmem_limit_bytes=20 << 20)


def direction_cosines(count):
    order = jnp.arange(count, dtype=jnp.int32).astype(jnp.float32)
    height = 1.0 - (2.0 * order + 1.0) / count
    radial = jnp.sqrt(1.0 - height * height)
    azimuth = order * golden_turn
    return (radial * jnp.cos(azimuth), radial * jnp.sin(azimuth), height)


def phase_angles(points, count):
    dir_x, dir_y, dir_z = direction_cosines(count)
    return wave_number * (
        points[0][:, None] * dir_x[None, :]
        + points[1][:, None] * dir_y[None, :]
        + points[2][:, None] * dir_z[None, :]
    )


def far_matrix(centers, near_mask):
    total_boxes = centers.shape[1]
    squared = jnp.zeros((total_boxes, total_boxes), jnp.float32)
    for axis_number in range(3):
        spread = centers[axis_number][:, None] - centers[axis_number][None, :]
        squared = squared + spread * spread
    spacing = jnp.sqrt(1.0 + squared)
    kernel = jnp.cos(wave_number * spacing) / (1.0 + spacing) * (far_gain / math.sqrt(total_boxes))
    rows = jnp.arange(total_boxes, dtype=jnp.int32)[:, None]
    cols = jnp.arange(total_boxes, dtype=jnp.int32)[None, :]
    linked = (
        (cols == rows)
        | (cols == rows - 1) & (near_mask[0][:, None] == 1)
        | (cols == rows + 1) & (near_mask[1][:, None] == 1)
    )
    return jnp.where(linked, 0.0, kernel).astype(jnp.bfloat16)


def swap_matrix(outer, inner):
    size = outer * inner
    row = lax.broadcasted_iota(jnp.int32, (size, size), 0)
    col = lax.broadcasted_iota(jnp.int32, (size, size), 1)
    source = lax.rem(row, inner) * outer + lax.div(row, inner)
    return jnp.where(source == col, 1.0, 0.0).astype(jnp.bfloat16)


def held(value):
    return pltpu.with_memory_space_constraint(value, pltpu.VMEM)


def far_away(value):
    return pltpu.with_memory_space_constraint(value, pltpu.HBM)


def pack_body(currents_ref, *refs, devices, angles_each, group):
    outs, (loaded_ref, turned_ref, mixed_ref, load_sems, store_sems) = refs[:-5], refs[-5:]
    boxes, _, unknowns, angles = currents_ref.shape
    rows = 2 * boxes
    loads = [
        pltpu.make_async_copy(currents_ref.at[box], loaded_ref.at[box], load_sems.at[box])
        for box in range(boxes)
    ]
    for load in loads:
        load.start()
    swap = swap_matrix(group, rows)
    for box, load in enumerate(loads):
        load.wait()
        for part in range(2):
            turned_ref[part * boxes + box] = loaded_ref[box, part].T
    per_out = angles_each // len(outs)
    stores = []
    for number, first in enumerate(range(0, angles, group)):
        own, device = divmod(first, devices)
        tile = turned_ref[:, first : first + group, :].reshape(rows * group, unknowns)
        mixed = jnp.dot(swap, tile, preferred_element_type=jnp.float32)
        mixed_ref[number] = mixed.astype(jnp.bfloat16).reshape(group, rows, unknowns)
        which, slot = divmod(own, per_out)
        target = outs[which].at[pl.ds(device, group), slot]
        store = pltpu.make_async_copy(mixed_ref.at[number], target, store_sems.at[number])
        store.start()
        stores.append(store)
    for store in stores:
        store.wait()


def pack(currents, devices, chunks):
    boxes, _, unknowns, angles = currents.shape
    angles_each = angles // devices
    group = math.gcd(16, devices)
    rows = 2 * boxes
    body = functools.partial(pack_body, devices=devices, angles_each=angles_each, group=group)
    shape = jax.ShapeDtypeStruct((devices, angles_each // chunks, rows, unknowns), jnp.bfloat16)
    return pl.pallas_call(
        body,
        in_specs=[hbm],
        out_specs=[hbm] * chunks,
        out_shape=[shape] * chunks,
        scratch_shapes=[
            pltpu.VMEM(currents.shape, jnp.bfloat16),
            pltpu.VMEM((rows, angles, unknowns), jnp.bfloat16),
            pltpu.VMEM((angles // group, group, rows, unknowns), jnp.bfloat16),
            pltpu.SemaphoreType.DMA((boxes,)),
            pltpu.SemaphoreType.DMA((angles // group,)),
        ],
        compiler_params=params,
        name="pack",
    )(far_away(currents))


def unpack_body(near_ref, *refs, devices, angles_each, group):
    ins, (out_ref, loaded_ref, turned_ref, done_ref, load_sems, store_sems) = refs[:-6], refs[-6:]
    boxes, _, unknowns, angles = near_ref.shape
    rows = 2 * boxes
    per_in = angles_each // len(ins)
    loads = []
    for number, first in enumerate(range(0, angles, group)):
        own, device = divmod(first, devices)
        which, slot = divmod(own, per_in)
        source = ins[which].at[pl.ds(device, group), slot]
        loads.append(pltpu.make_async_copy(source, loaded_ref.at[number], load_sems.at[number]))
    for load in loads:
        load.start()
    swap = swap_matrix(rows, group)
    for number, load in enumerate(loads):
        load.wait()
        tile = loaded_ref[number].reshape(rows * group, unknowns)
        mixed = jnp.dot(swap, tile, preferred_element_type=jnp.float32)
        turned_ref[:, number * group : (number + 1) * group, :] = mixed.astype(
            jnp.bfloat16
        ).reshape(rows, group, unknowns)
    stores = [
        pltpu.make_async_copy(done_ref.at[box], out_ref.at[box], store_sems.at[box])
        for box in range(boxes)
    ]
    for box, store in enumerate(stores):
        for part in range(2):
            far = turned_ref[part * boxes + box].T.astype(jnp.float32)
            done_ref[box, part] = (near_ref[box, part] + far).astype(jnp.bfloat16)
        store.start()
    for store in stores:
        store.wait()


def unpack(near, pieces, devices):
    boxes, _, unknowns, angles = near.shape
    angles_each = angles // devices
    group = math.gcd(16, devices)
    rows = 2 * boxes
    body = functools.partial(unpack_body, devices=devices, angles_each=angles_each, group=group)
    return pl.pallas_call(
        body,
        in_specs=[vmem] + [hbm] * len(pieces),
        out_specs=hbm,
        out_shape=jax.ShapeDtypeStruct(near.shape, jnp.bfloat16),
        scratch_shapes=[
            pltpu.VMEM((angles // group, group, rows, unknowns), jnp.bfloat16),
            pltpu.VMEM((rows, angles, unknowns), jnp.bfloat16),
            pltpu.VMEM(near.shape, jnp.bfloat16),
            pltpu.SemaphoreType.DMA((angles // group,)),
            pltpu.SemaphoreType.DMA((boxes,)),
        ],
        compiler_params=params,
        name="unpack",
    )(held(near), *[far_away(x) for x in pieces])


def far_body(
    arrived_ref, gather_hbm, spread_hbm, translate_ref, cos_ref, sin_ref, out_ref,
    gather_ref, spread_ref, pat_ref, rec_ref, done_ref, load_sems, sems,
):
    devices, slots, rows, unknowns = arrived_ref.shape
    boxes = rows // 2
    total, count = cos_ref.shape
    width = math.gcd(count, 256)
    loads = []
    for number, low in enumerate(range(0, count, width)):
        piece = (slice(None), slice(None), pl.ds(low, width))
        loads.append(
            pltpu.make_async_copy(
                gather_hbm.at[piece], gather_ref.at[piece], load_sems.at[number]
            )
        )
    loads.append(pltpu.make_async_copy(spread_hbm, spread_ref, load_sems.at[len(loads)]))
    for load in loads:
        load.start()
    some = math.gcd(devices, max(1, far_rows // (slots * rows)))

    def product(left, right):
        return jnp.dot(left, right, preferred_element_type=jnp.float32)

    for number, low in enumerate(range(0, count, width)):
        high = low + width
        loads[number].wait()
        for first in range(0, devices, some):
            arrived = arrived_ref[first : first + some].reshape(some * slots * rows, unknowns)
            span = slice(first * boxes, (first + some) * boxes)
            shape = (some, slots, 2, boxes, width)
            by_re = product(arrived, gather_ref[0, :, low:high]).reshape(shape)
            by_im = product(arrived, gather_ref[1, :, low:high]).reshape(shape)
            cosine = cos_ref[span, low:high].reshape(some, boxes, width)
            sine = sin_ref[span, low:high].reshape(some, boxes, width)
            for slot in range(slots):
                pat_re = by_re[:, slot, 0] - by_im[:, slot, 1]
                pat_im = by_re[:, slot, 1] + by_im[:, slot, 0]
                out_re = (cosine * pat_re + sine * pat_im).reshape(some * boxes, width)
                out_im = (cosine * pat_im - sine * pat_re).reshape(some * boxes, width)
                pat_ref[slot, span, low:high] = out_re.astype(jnp.bfloat16)
                pat_ref[slot, span, count + low : count + high] = out_im.astype(jnp.bfloat16)
    loads[-1].wait()
    stores = []
    pairs = math.gcd(slots, far_slots)
    for begin in range(0, slots, pairs):
        for slot in range(begin, begin + pairs):
            for low in range(0, count, width):
                high = low + width
                translate = translate_ref[...]
                sum_re = product(translate, pat_ref[slot, :, low:high])
                sum_im = product(translate, pat_ref[slot, :, count + low : count + high])
                cosine = cos_ref[:, low:high]
                sine = sin_ref[:, low:high]
                rec_re = (cosine * sum_re - sine * sum_im).astype(jnp.bfloat16)
                rec_im = (cosine * sum_im + sine * sum_re).astype(jnp.bfloat16)
                rec_ref[slot, :, low:high] = rec_re
                rec_ref[slot, :, count + low : count + high] = rec_im
                rec_ref[slot, :, 2 * count + low : 2 * count + high] = -rec_re
        many = pairs * total
        whole = (pairs, devices, 1, boxes, unknowns)
        rec_re_im = rec_ref[begin : begin + pairs, :, : 2 * count].reshape(many, 2 * count)
        rec_im_re = rec_ref[begin : begin + pairs, :, count:].reshape(many, 2 * count)
        imag = product(rec_re_im, spread_ref[...]).reshape(whole)
        real = product(rec_im_re, spread_ref[...]).reshape(whole)
        both = jnp.concatenate([-real, imag], 2).reshape(pairs, devices, rows, unknowns)
        done_ref[begin : begin + pairs] = both.astype(jnp.bfloat16)
        for slot in range(begin, begin + pairs):
            store = pltpu.make_async_copy(done_ref.at[slot], out_ref.at[:, slot], sems.at[slot])
            store.start()
            stores.append(store)
    for store in stores:
        store.wait()


def far_field(arrived, gather, spread, translate, cosine, sine):
    devices, slots, rows, unknowns = arrived.shape
    total, count = cosine.shape
    return pl.pallas_call(
        far_body,
        in_specs=[vmem, hbm, hbm, vmem, vmem, vmem],
        out_specs=hbm,
        out_shape=jax.ShapeDtypeStruct(arrived.shape, jnp.bfloat16),
        scratch_shapes=[
            pltpu.VMEM(gather.shape, jnp.bfloat16),
            pltpu.VMEM(spread.shape, jnp.bfloat16),
            pltpu.VMEM((slots, total, 2 * count), jnp.bfloat16),
            pltpu.VMEM((slots, total, 3 * count), jnp.bfloat16),
            pltpu.VMEM((slots, devices, rows, unknowns), jnp.bfloat16),
            pltpu.SemaphoreType.DMA((1 + count // math.gcd(count, 256),)),
            pltpu.SemaphoreType.DMA((slots,)),
        ],
        compiler_params=params,
        name="far",
    )(held(arrived), far_away(gather), far_away(spread), *[held(x) for x in (translate, cosine, sine)])


def near_body(place_ref, mask_ref, currents_ref, low_ref, high_ref, blocks_ref, out_ref):
    boxes, _, unknowns, angles = currents_ref.shape
    box = pl.program_id(0)
    own = place_ref[0] * boxes + box

    def both(block):
        return jnp.concatenate([block[0], block[1]], 1)

    zero = jnp.zeros((unknowns, 2 * angles), jnp.bfloat16)
    here = both(currents_ref[box])
    before = jnp.where(box == 0, both(low_ref[0]), both(currents_ref[jnp.maximum(box - 1, 0)]))
    after = jnp.where(
        box == boxes - 1, both(high_ref[0]), both(currents_ref[jnp.minimum(box + 1, boxes - 1)])
    )
    before = jnp.where(mask_ref[0, own] == 1, before, zero)
    after = jnp.where(mask_ref[1, own] == 1, after, zero)
    by_re = jnp.zeros((unknowns, 2 * angles), jnp.float32)
    by_im = jnp.zeros((unknowns, 2 * angles), jnp.float32)
    for which, vectors in enumerate((here, before, after)):
        by_re += jnp.dot(blocks_ref[0, which, 0], vectors, preferred_element_type=jnp.float32)
        by_im += jnp.dot(blocks_ref[0, which, 1], vectors, preferred_element_type=jnp.float32)
    out_ref[box, 0] = by_re[:, :angles] - by_im[:, angles:]
    out_ref[box, 1] = by_re[:, angles:] + by_im[:, :angles]


def near_field(currents, low, high, near_blocks, near_mask, place):
    boxes, _, unknowns, _ = currents.shape
    return pl.pallas_call(
        near_body,
        grid_spec=pltpu.PrefetchScalarGridSpec(
            num_scalar_prefetch=2,
            grid=(boxes,),
            in_specs=[
                vmem,
                vmem,
                vmem,
                pl.BlockSpec((1, 3, 2, unknowns, unknowns), lambda i, *_: (i, 0, 0, 0, 0)),
            ],
            out_specs=vmem,
        ),
        out_shape=pltpu.VMEM(currents.shape, jnp.float32),
        compiler_params=params,
        name="near",
    )(place, near_mask, held(currents), held(low), held(high), near_blocks)


def edges(currents):
    count = lax.axis_size(axes)
    forward = [(i, i + 1) for i in range(count - 1)]
    backward = [(i + 1, i) for i in range(count - 1)]
    low = lax.ppermute(currents[-1:], axes, forward)
    high = lax.ppermute(currents[:1], axes, backward)
    return low, high


def exchange(value):
    return lax.all_to_all(value, axes, split_axis=0, concat_axis=0, tiled=True)


def product(currents, near_blocks, near_mask, aggregate, disaggregate, centers):
    devices = lax.axis_size(axes)
    angles_each = currents.shape[3] // devices
    chunks = math.gcd(chunks_wanted, angles_each)
    dir_count = aggregate.shape[1]
    place = lax.axis_index(axes).astype(jnp.int32).reshape(1)

    packed = pack(currents, devices, chunks)
    arrived = [exchange(x) for x in packed]
    low, high = edges(currents)
    gather = aggregate.transpose(0, 2, 1)
    turned = disaggregate.transpose(0, 2, 1)
    spread = jnp.concatenate([turned[1], turned[0]], 0)
    translate = far_matrix(centers, near_mask)
    theta = phase_angles(centers, dir_count)
    cosine = jnp.cos(theta)
    sine = jnp.sin(theta)
    far = [far_field(x, gather, spread, translate, cosine, sine) for x in arrived]
    pieces = [exchange(x) for x in far]
    near = near_field(currents, low, high, near_blocks, near_mask, place)
    return unpack(near, pieces, devices)


def solution(mesh):
    return jax.shard_map(
        product,
        mesh=mesh,
        in_specs=(
            P(axes, None, None, None),
            P(axes, None, None, None, None),
            P(),
            P(),
            P(),
            P(),
        ),
        out_specs=P(axes, None, None, None),
        check_vma=False,
    )
```

```python
import functools
import math

import jax
import jax.numpy as jnp
from jax import lax
from jax.experimental import pallas as pl
from jax.experimental.pallas import tpu as pltpu
from jax.sharding import Mesh, PartitionSpec as P


wave_number = 2.0
far_gain = 8.0
golden_turn = 2.399963229728653
axes = ("outer", "core", "far", "close")
route = ("outer", "close", "core", "far")
chunks_wanted = 1
far_rows = 512
pack_waits = 4
far_slots = 1
hbm = pl.BlockSpec(memory_space=pltpu.HBM)
vmem = pl.BlockSpec(memory_space=pltpu.VMEM)
params = pltpu.CompilerParams(vmem_limit_bytes=20 << 20)


def direction_cosines(count):
    order = jnp.arange(count, dtype=jnp.int32).astype(jnp.float32)
    height = 1.0 - (2.0 * order + 1.0) / count
    radial = jnp.sqrt(1.0 - height * height)
    azimuth = order * golden_turn
    return (radial * jnp.cos(azimuth), radial * jnp.sin(azimuth), height)


def phase_angles(points, count):
    dir_x, dir_y, dir_z = direction_cosines(count)
    return wave_number * (
        points[0][:, None] * dir_x[None, :]
        + points[1][:, None] * dir_y[None, :]
        + points[2][:, None] * dir_z[None, :]
    )


def far_matrix(centers, near_mask, names):
    total_boxes = centers.shape[1]
    squared = jnp.zeros((total_boxes, total_boxes), jnp.float32)
    for axis_number in range(3):
        spread = centers[axis_number][:, None] - centers[axis_number][None, :]
        squared = squared + spread * spread
    spacing = jnp.sqrt(1.0 + squared)
    kernel = jnp.cos(wave_number * spacing) / (1.0 + spacing) * (far_gain / math.sqrt(total_boxes))
    rows = names[:, None]
    cols = names[None, :]
    linked = (
        (cols == rows)
        | (cols == rows - 1) & (near_mask[0][:, None] == 1)
        | (cols == rows + 1) & (near_mask[1][:, None] == 1)
    )
    return jnp.where(linked, 0.0, kernel).astype(jnp.bfloat16)


def swap_matrix(outer, inner):
    size = outer * inner
    row = lax.broadcasted_iota(jnp.int32, (size, size), 0)
    col = lax.broadcasted_iota(jnp.int32, (size, size), 1)
    source = lax.rem(row, inner) * outer + lax.div(row, inner)
    return jnp.where(source == col, 1.0, 0.0).astype(jnp.bfloat16)


def held(value):
    return pltpu.with_memory_space_constraint(value, pltpu.VMEM)


def far_away(value):
    return pltpu.with_memory_space_constraint(value, pltpu.HBM)


def pack_body(currents_ref, *refs, devices, angles_each, group):
    outs, (loaded_ref, turned_ref, mixed_ref, load_sems, store_sems) = refs[:-5], refs[-5:]
    boxes, _, unknowns, angles = currents_ref.shape
    rows = 2 * boxes
    loads = [
        pltpu.make_async_copy(currents_ref.at[box], loaded_ref.at[box], load_sems.at[box])
        for box in range(boxes)
    ]
    for load in loads:
        load.start()
    swap = swap_matrix(group, rows)
    for box in range(boxes):
        if box % pack_waits == 0:
            for load in loads[box : box + pack_waits]:
                load.wait()
        for part in range(2):
            turned_ref[part * boxes + box] = loaded_ref[box, part].T
    per_out = angles_each // len(outs)
    stores = []
    for number, first in enumerate(range(0, angles, group)):
        own, device = divmod(first, devices)
        tile = turned_ref[:, first : first + group, :].reshape(rows * group, unknowns)
        mixed = jnp.dot(swap, tile, preferred_element_type=jnp.float32)
        mixed_ref[number] = mixed.astype(jnp.bfloat16).reshape(group, rows, unknowns)
        which, slot = divmod(own, per_out)
        target = outs[which].at[pl.ds(device, group), slot]
        store = pltpu.make_async_copy(mixed_ref.at[number], target, store_sems.at[number])
        store.start()
        stores.append(store)
    for store in stores:
        store.wait()


def pack(currents, devices, chunks):
    boxes, _, unknowns, angles = currents.shape
    angles_each = angles // devices
    group = math.gcd(16, devices)
    rows = 2 * boxes
    body = functools.partial(pack_body, devices=devices, angles_each=angles_each, group=group)
    shape = jax.ShapeDtypeStruct((devices, angles_each // chunks, rows, unknowns), jnp.bfloat16)
    return pl.pallas_call(
        body,
        in_specs=[hbm],
        out_specs=[hbm] * chunks,
        out_shape=[shape] * chunks,
        scratch_shapes=[
            pltpu.VMEM(currents.shape, jnp.bfloat16),
            pltpu.VMEM((rows, angles, unknowns), jnp.bfloat16),
            pltpu.VMEM((angles // group, group, rows, unknowns), jnp.bfloat16),
            pltpu.SemaphoreType.DMA((boxes,)),
            pltpu.SemaphoreType.DMA((angles // group,)),
        ],
        compiler_params=params,
        name="pack",
    )(far_away(currents))


def unpack_body(near_ref, *refs, devices, angles_each, group):
    ins, (out_ref, turned_ref, done_ref, sems) = refs[:-4], refs[-4:]
    boxes, _, unknowns, angles = near_ref.shape
    rows = 2 * boxes
    per_in = angles_each // len(ins)
    swap = swap_matrix(rows, group)
    for first in range(0, angles, group):
        own, device = divmod(first, devices)
        which, slot = divmod(own, per_in)
        tile = ins[which][device : device + group, slot].reshape(rows * group, unknowns)
        mixed = jnp.dot(swap, tile, preferred_element_type=jnp.float32)
        turned_ref[:, first : first + group, :] = mixed.astype(jnp.bfloat16).reshape(
            rows, group, unknowns
        )
    stores = [
        pltpu.make_async_copy(done_ref.at[box], out_ref.at[box], sems.at[box])
        for box in range(boxes)
    ]
    for box, store in enumerate(stores):
        for part in range(2):
            far = turned_ref[part * boxes + box].T.astype(jnp.float32)
            near = near_ref[box, part].astype(jnp.float32)
            done_ref[box, part] = (near + far).astype(jnp.bfloat16)
        store.start()
    for store in stores:
        store.wait()


def unpack(near, pieces, devices):
    boxes, _, unknowns, angles = near.shape
    angles_each = angles // devices
    group = math.gcd(16, devices)
    rows = 2 * boxes
    body = functools.partial(unpack_body, devices=devices, angles_each=angles_each, group=group)
    return pl.pallas_call(
        body,
        in_specs=[vmem] * (1 + len(pieces)),
        out_specs=hbm,
        out_shape=jax.ShapeDtypeStruct(near.shape, jnp.bfloat16),
        scratch_shapes=[
            pltpu.VMEM((rows, angles, unknowns), jnp.bfloat16),
            pltpu.VMEM(near.shape, jnp.bfloat16),
            pltpu.SemaphoreType.DMA((boxes,)),
        ],
        compiler_params=params,
        name="unpack",
    )(held(near), *[held(x) for x in pieces])


def far_body(
    arrived_ref, gather_ref, gather_hbm, spread_hbm, translate_ref, cos_ref, sin_ref, out_ref,
    later_ref, spread_ref, pat_ref, rec_ref, done_ref, later_sem, load_sem, sems,
):
    devices, slots, rows, unknowns = arrived_ref.shape
    boxes = rows // 2
    total, count = cos_ref.shape
    width = gather_ref.shape[2]
    later = pltpu.make_async_copy(gather_hbm, later_ref, later_sem)
    later.start()
    load = pltpu.make_async_copy(spread_hbm, spread_ref, load_sem)
    load.start()
    some = math.gcd(devices, max(1, far_rows // (slots * rows)))

    def product(left, right):
        return jnp.dot(left, right, preferred_element_type=jnp.float32)

    for low in range(0, count, width):
        high = low + width
        table_ref = later_ref if low else gather_ref
        start = max(0, low - width)
        if low == width:
            later.wait()
        for first in range(0, devices, some):
            arrived = arrived_ref[first : first + some].reshape(some * slots * rows, unknowns)
            span = slice(first * boxes, (first + some) * boxes)
            shape = (some, slots, 2, boxes, width)
            by_re = product(arrived, table_ref[0, :, start : start + width]).reshape(shape)
            by_im = product(arrived, table_ref[1, :, start : start + width]).reshape(shape)
            cosine = cos_ref[span, low:high].reshape(some, boxes, width)
            sine = sin_ref[span, low:high].reshape(some, boxes, width)
            for slot in range(slots):
                pat_re = by_re[:, slot, 0] - by_im[:, slot, 1]
                pat_im = by_re[:, slot, 1] + by_im[:, slot, 0]
                out_re = (cosine * pat_re + sine * pat_im).reshape(some * boxes, width)
                out_im = (cosine * pat_im - sine * pat_re).reshape(some * boxes, width)
                pat_ref[slot, span, low:high] = out_re.astype(jnp.bfloat16)
                pat_ref[slot, span, count + low : count + high] = out_im.astype(jnp.bfloat16)
    load.wait()
    stores = []
    pairs = math.gcd(slots, far_slots)
    for begin in range(0, slots, pairs):
        for slot in range(begin, begin + pairs):
            for low in range(0, count, width):
                high = low + width
                translate = translate_ref[...]
                sum_re = product(translate, pat_ref[slot, :, low:high])
                sum_im = product(translate, pat_ref[slot, :, count + low : count + high])
                cosine = cos_ref[:, low:high]
                sine = sin_ref[:, low:high]
                rec_re = (cosine * sum_re - sine * sum_im).astype(jnp.bfloat16)
                rec_im = (cosine * sum_im + sine * sum_re).astype(jnp.bfloat16)
                rec_ref[slot, :, low:high] = rec_re
                rec_ref[slot, :, count + low : count + high] = rec_im
                rec_ref[slot, :, 2 * count + low : 2 * count + high] = -rec_re
        many = pairs * total
        whole = (pairs, devices, 1, boxes, unknowns)
        rec_re_im = rec_ref[begin : begin + pairs, :, : 2 * count].reshape(many, 2 * count)
        rec_im_re = rec_ref[begin : begin + pairs, :, count:].reshape(many, 2 * count)
        imag = product(rec_re_im, spread_ref[...]).reshape(whole)
        real = product(rec_im_re, spread_ref[...]).reshape(whole)
        both = jnp.concatenate([-real, imag], 2).reshape(pairs, devices, rows, unknowns)
        done_ref[begin : begin + pairs] = both.astype(jnp.bfloat16)
        for slot in range(begin, begin + pairs):
            store = pltpu.make_async_copy(done_ref.at[slot], out_ref.at[:, slot], sems.at[slot])
            store.start()
            stores.append(store)
    for store in stores:
        store.wait()


def far_field(arrived, gather, spread, translate, cosine, sine):
    devices, slots, rows, unknowns = arrived.shape
    total, count = cosine.shape
    width = math.gcd(count // 2, 256)
    later = gather[:, :, width:]
    return pl.pallas_call(
        far_body,
        in_specs=[vmem, vmem, hbm, hbm, vmem, vmem, vmem],
        out_specs=hbm,
        out_shape=jax.ShapeDtypeStruct(arrived.shape, jnp.bfloat16),
        scratch_shapes=[
            pltpu.VMEM(later.shape, jnp.bfloat16),
            pltpu.VMEM(spread.shape, jnp.bfloat16),
            pltpu.VMEM((slots, total, 2 * count), jnp.bfloat16),
            pltpu.VMEM((slots, total, 3 * count), jnp.bfloat16),
            pltpu.VMEM((slots, devices, rows, unknowns), jnp.bfloat16),
            pltpu.SemaphoreType.DMA(()),
            pltpu.SemaphoreType.DMA(()),
            pltpu.SemaphoreType.DMA((slots,)),
        ],
        compiler_params=params,
        name="far",
    )(held(arrived), held(gather[:, :, :width]), far_away(later), far_away(spread), *[held(x) for x in (translate, cosine, sine)])


def near_body(place_ref, mask_ref, currents_ref, low_ref, high_ref, blocks_ref, out_ref):
    boxes, _, unknowns, angles = currents_ref.shape
    box = pl.program_id(0)
    own = place_ref[0] * boxes + box

    def both(block):
        return jnp.concatenate([block[0], block[1]], 1)

    zero = jnp.zeros((unknowns, 2 * angles), jnp.bfloat16)
    here = both(currents_ref[box])
    before = jnp.where(box == 0, both(low_ref[0]), both(currents_ref[jnp.maximum(box - 1, 0)]))
    after = jnp.where(
        box == boxes - 1, both(high_ref[0]), both(currents_ref[jnp.minimum(box + 1, boxes - 1)])
    )
    before = jnp.where(mask_ref[0, own] == 1, before, zero)
    after = jnp.where(mask_ref[1, own] == 1, after, zero)
    by_re = jnp.zeros((unknowns, 2 * angles), jnp.float32)
    by_im = jnp.zeros((unknowns, 2 * angles), jnp.float32)
    for which, vectors in enumerate((here, before, after)):
        by_re += jnp.dot(blocks_ref[0, which, 0], vectors, preferred_element_type=jnp.float32)
        by_im += jnp.dot(blocks_ref[0, which, 1], vectors, preferred_element_type=jnp.float32)
    out_ref[box, 0] = (by_re[:, :angles] - by_im[:, angles:]).astype(jnp.bfloat16)
    out_ref[box, 1] = (by_re[:, angles:] + by_im[:, :angles]).astype(jnp.bfloat16)


def near_field(currents, low, high, near_blocks, near_mask, place):
    boxes, _, unknowns, _ = currents.shape
    return pl.pallas_call(
        near_body,
        grid_spec=pltpu.PrefetchScalarGridSpec(
            num_scalar_prefetch=2,
            grid=(boxes,),
            in_specs=[
                vmem,
                vmem,
                vmem,
                pl.BlockSpec((1, 3, 2, unknowns, unknowns), lambda i, *_: (i, 0, 0, 0, 0)),
            ],
            out_specs=vmem,
        ),
        out_shape=pltpu.VMEM(currents.shape, jnp.bfloat16),
        compiler_params=params,
        name="near",
    )(place, near_mask, currents, low, high, near_blocks)


def edges(currents):
    count = lax.axis_size(axes)
    forward = [(i, i + 1) for i in range(count - 1)]
    backward = [(i + 1, i) for i in range(count - 1)]
    low = lax.ppermute(far_away(currents[-1:]), axes, forward)
    high = lax.ppermute(far_away(currents[:1]), axes, backward)
    return low, high


def routed(values):
    sizes = [lax.axis_size(axis) for axis in axes]
    split = values.reshape(values.shape[:-1] + (*sizes, -1))
    lead = values.ndim - 1
    order = [*range(lead), *(lead + axes.index(axis) for axis in route), lead + len(axes)]
    return split.transpose(order).reshape(values.shape)


def exchange(value):
    return lax.all_to_all(value, route, split_axis=0, concat_axis=0, tiled=True)


def product(currents, near_blocks, near_mask, aggregate, disaggregate, centers):
    devices = lax.axis_size(axes)
    angles_each = currents.shape[3] // devices
    chunks = math.gcd(chunks_wanted, angles_each)
    dir_count = aggregate.shape[1]
    place = lax.axis_index(axes).astype(jnp.int32).reshape(1)

    packed = pack(currents, devices, chunks)
    arrived = [exchange(x) for x in packed]
    low, high = edges(currents)
    gather = aggregate.transpose(0, 2, 1)
    turned = disaggregate.transpose(0, 2, 1)
    spread = jnp.concatenate([turned[1], turned[0]], 0)
    names = jnp.arange(centers.shape[1], dtype=jnp.int32)
    points = routed(centers)
    translate = far_matrix(points, routed(near_mask), routed(names))
    theta = phase_angles(points, dir_count)
    cosine = jnp.cos(theta)
    sine = jnp.sin(theta)
    far = [far_field(x, gather, spread, translate, cosine, sine) for x in arrived]
    pieces = [exchange(x) for x in far]
    near = near_field(currents, low, high, near_blocks, near_mask, place)
    return unpack(near, pieces, devices)


def solution(mesh):
    box, direction = (mesh.shape[axis] for axis in ("box", "dir"))
    core = math.gcd(box, 2)
    close = math.gcd(direction, 2)
    shape = (box // core, core, direction // close, close)
    finer = Mesh(mesh.devices.reshape(shape), axes)
    return jax.shard_map(
        product,
        mesh=finer,
        in_specs=(
            P(axes, None, None, None),
            P(axes, None, None, None, None),
            P(),
            P(),
            P(),
            P(),
        ),
        out_specs=P(axes, None, None, None),
        check_vma=False,
    )
```

```python
import functools
import math

import jax
import jax.numpy as jnp
from jax import lax
from jax.experimental import pallas as pl
from jax.experimental.pallas import tpu as pltpu
from jax.sharding import PartitionSpec as P


wave_number = 2.0
far_gain = 8.0
golden_turn = 2.399963229728653
axes = ("box", "dir")
route = ("dir", "box")
chunks_wanted = 1
far_rows = 512
pack_waits = 4
far_slots = 1
hbm = pl.BlockSpec(memory_space=pltpu.HBM)
vmem = pl.BlockSpec(memory_space=pltpu.VMEM)
params = pltpu.CompilerParams(vmem_limit_bytes=20 << 20)


def direction_cosines(count):
    order = jnp.arange(count, dtype=jnp.int32).astype(jnp.float32)
    height = 1.0 - (2.0 * order + 1.0) / count
    radial = jnp.sqrt(1.0 - height * height)
    azimuth = order * golden_turn
    return (radial * jnp.cos(azimuth), radial * jnp.sin(azimuth), height)


def phase_angles(points, count):
    dir_x, dir_y, dir_z = direction_cosines(count)
    return wave_number * (
        points[0][:, None] * dir_x[None, :]
        + points[1][:, None] * dir_y[None, :]
        + points[2][:, None] * dir_z[None, :]
    )


def far_matrix(centers, near_mask, names):
    total_boxes = centers.shape[1]
    squared = jnp.zeros((total_boxes, total_boxes), jnp.float32)
    for axis_number in range(3):
        spread = centers[axis_number][:, None] - centers[axis_number][None, :]
        squared = squared + spread * spread
    spacing = jnp.sqrt(1.0 + squared)
    kernel = jnp.cos(wave_number * spacing) / (1.0 + spacing) * (far_gain / math.sqrt(total_boxes))
    rows = names[:, None]
    cols = names[None, :]
    linked = (
        (cols == rows)
        | (cols == rows - 1) & (near_mask[0][:, None] == 1)
        | (cols == rows + 1) & (near_mask[1][:, None] == 1)
    )
    return jnp.where(linked, 0.0, kernel).astype(jnp.bfloat16)


def swap_matrix(outer, inner):
    size = outer * inner
    row = lax.broadcasted_iota(jnp.int32, (size, size), 0)
    col = lax.broadcasted_iota(jnp.int32, (size, size), 1)
    source = lax.rem(row, inner) * outer + lax.div(row, inner)
    return jnp.where(source == col, 1.0, 0.0).astype(jnp.bfloat16)


def held(value):
    return pltpu.with_memory_space_constraint(value, pltpu.VMEM)


def far_away(value):
    return pltpu.with_memory_space_constraint(value, pltpu.HBM)


def pack_body(currents_ref, *refs, devices, angles_each, group):
    outs, (loaded_ref, turned_ref, mixed_ref, load_sems, store_sems) = refs[:-5], refs[-5:]
    boxes, _, unknowns, angles = currents_ref.shape
    rows = 2 * boxes
    loads = [
        pltpu.make_async_copy(currents_ref.at[box], loaded_ref.at[box], load_sems.at[box])
        for box in range(boxes)
    ]
    for load in loads:
        load.start()
    swap = swap_matrix(group, rows)
    for box in range(boxes):
        if box % pack_waits == 0:
            for load in loads[box : box + pack_waits]:
                load.wait()
        for part in range(2):
            turned_ref[part * boxes + box] = loaded_ref[box, part].T
    per_out = angles_each // len(outs)
    stores = []
    for number, first in enumerate(range(0, angles, group)):
        own, device = divmod(first, devices)
        tile = turned_ref[:, first : first + group, :].reshape(rows * group, unknowns)
        mixed = jnp.dot(swap, tile, preferred_element_type=jnp.float32)
        mixed_ref[number] = mixed.astype(jnp.bfloat16).reshape(group, rows, unknowns)
        which, slot = divmod(own, per_out)
        target = outs[which].at[pl.ds(device, group), slot]
        store = pltpu.make_async_copy(mixed_ref.at[number], target, store_sems.at[number])
        store.start()
        stores.append(store)
    for store in stores:
        store.wait()


def pack(currents, devices, chunks):
    boxes, _, unknowns, angles = currents.shape
    angles_each = angles // devices
    group = math.gcd(16, devices)
    rows = 2 * boxes
    body = functools.partial(pack_body, devices=devices, angles_each=angles_each, group=group)
    shape = jax.ShapeDtypeStruct((devices, angles_each // chunks, rows, unknowns), jnp.bfloat16)
    return pl.pallas_call(
        body,
        in_specs=[hbm],
        out_specs=[hbm] * chunks,
        out_shape=[shape] * chunks,
        scratch_shapes=[
            pltpu.VMEM(currents.shape, jnp.bfloat16),
            pltpu.VMEM((rows, angles, unknowns), jnp.bfloat16),
            pltpu.VMEM((angles // group, group, rows, unknowns), jnp.bfloat16),
            pltpu.SemaphoreType.DMA((boxes,)),
            pltpu.SemaphoreType.DMA((angles // group,)),
        ],
        compiler_params=params,
        name="pack",
    )(far_away(currents))


def unpack_body(near_ref, *refs, devices, angles_each, group):
    ins, (out_ref, turned_ref, done_ref, sems) = refs[:-4], refs[-4:]
    boxes, _, unknowns, angles = near_ref.shape
    rows = 2 * boxes
    per_in = angles_each // len(ins)
    swap = swap_matrix(rows, group)
    for first in range(0, angles, group):
        own, device = divmod(first, devices)
        which, slot = divmod(own, per_in)
        tile = ins[which][device : device + group, slot].reshape(rows * group, unknowns)
        mixed = jnp.dot(swap, tile, preferred_element_type=jnp.float32)
        turned_ref[:, first : first + group, :] = mixed.astype(jnp.bfloat16).reshape(
            rows, group, unknowns
        )
    stores = [
        pltpu.make_async_copy(done_ref.at[box], out_ref.at[box], sems.at[box])
        for box in range(boxes)
    ]
    for box, store in enumerate(stores):
        for part in range(2):
            far = turned_ref[part * boxes + box].T.astype(jnp.float32)
            near = near_ref[box, part].astype(jnp.float32)
            done_ref[box, part] = (near + far).astype(jnp.bfloat16)
        store.start()
    for store in stores:
        store.wait()


def unpack(near, pieces, devices):
    boxes, _, unknowns, angles = near.shape
    angles_each = angles // devices
    group = math.gcd(16, devices)
    rows = 2 * boxes
    body = functools.partial(unpack_body, devices=devices, angles_each=angles_each, group=group)
    return pl.pallas_call(
        body,
        in_specs=[vmem] * (1 + len(pieces)),
        out_specs=hbm,
        out_shape=jax.ShapeDtypeStruct(near.shape, jnp.bfloat16),
        scratch_shapes=[
            pltpu.VMEM((rows, angles, unknowns), jnp.bfloat16),
            pltpu.VMEM(near.shape, jnp.bfloat16),
            pltpu.SemaphoreType.DMA((boxes,)),
        ],
        compiler_params=params,
        name="unpack",
    )(held(near), *[held(x) for x in pieces])


def far_body(
    arrived_ref, gather_ref, gather_hbm, spread_hbm, translate_ref, cos_ref, sin_ref, out_ref,
    later_ref, spread_ref, pat_ref, rec_ref, done_ref, later_sem, load_sem, sems,
):
    devices, slots, rows, unknowns = arrived_ref.shape
    boxes = rows // 2
    total, count = cos_ref.shape
    width = gather_ref.shape[2]
    later = pltpu.make_async_copy(gather_hbm, later_ref, later_sem)
    later.start()
    load = pltpu.make_async_copy(spread_hbm, spread_ref, load_sem)
    load.start()
    some = math.gcd(devices, max(1, far_rows // (slots * rows)))

    def product(left, right):
        return jnp.dot(left, right, preferred_element_type=jnp.float32)

    for low in range(0, count, width):
        high = low + width
        table_ref = later_ref if low else gather_ref
        start = max(0, low - width)
        if low == width:
            later.wait()
        for first in range(0, devices, some):
            arrived = arrived_ref[first : first + some].reshape(some * slots * rows, unknowns)
            span = slice(first * boxes, (first + some) * boxes)
            shape = (some, slots, 2, boxes, width)
            by_re = product(arrived, table_ref[0, :, start : start + width]).reshape(shape)
            by_im = product(arrived, table_ref[1, :, start : start + width]).reshape(shape)
            cosine = cos_ref[span, low:high].reshape(some, boxes, width)
            sine = sin_ref[span, low:high].reshape(some, boxes, width)
            for slot in range(slots):
                pat_re = by_re[:, slot, 0] - by_im[:, slot, 1]
                pat_im = by_re[:, slot, 1] + by_im[:, slot, 0]
                out_re = (cosine * pat_re + sine * pat_im).reshape(some * boxes, width)
                out_im = (cosine * pat_im - sine * pat_re).reshape(some * boxes, width)
                pat_ref[slot, span, low:high] = out_re.astype(jnp.bfloat16)
                pat_ref[slot, span, count + low : count + high] = out_im.astype(jnp.bfloat16)
    load.wait()
    stores = []
    pairs = math.gcd(slots, far_slots)
    for begin in range(0, slots, pairs):
        for slot in range(begin, begin + pairs):
            for low in range(0, count, width):
                high = low + width
                translate = translate_ref[...]
                sum_re = product(translate, pat_ref[slot, :, low:high])
                sum_im = product(translate, pat_ref[slot, :, count + low : count + high])
                cosine = cos_ref[:, low:high]
                sine = sin_ref[:, low:high]
                rec_re = (cosine * sum_re - sine * sum_im).astype(jnp.bfloat16)
                rec_im = (cosine * sum_im + sine * sum_re).astype(jnp.bfloat16)
                rec_ref[slot, :, low:high] = rec_re
                rec_ref[slot, :, count + low : count + high] = rec_im
                rec_ref[slot, :, 2 * count + low : 2 * count + high] = -rec_re
        many = pairs * total
        whole = (pairs, devices, 1, boxes, unknowns)
        rec_re_im = rec_ref[begin : begin + pairs, :, : 2 * count].reshape(many, 2 * count)
        rec_im_re = rec_ref[begin : begin + pairs, :, count:].reshape(many, 2 * count)
        imag = product(rec_re_im, spread_ref[...]).reshape(whole)
        real = product(rec_im_re, spread_ref[...]).reshape(whole)
        both = jnp.concatenate([-real, imag], 2).reshape(pairs, devices, rows, unknowns)
        done_ref[begin : begin + pairs] = both.astype(jnp.bfloat16)
        for slot in range(begin, begin + pairs):
            store = pltpu.make_async_copy(done_ref.at[slot], out_ref.at[:, slot], sems.at[slot])
            store.start()
            stores.append(store)
    for store in stores:
        store.wait()


def far_field(arrived, gather, spread, translate, cosine, sine):
    devices, slots, rows, unknowns = arrived.shape
    total, count = cosine.shape
    width = math.gcd(count // 2, 256)
    later = gather[:, :, width:]
    return pl.pallas_call(
        far_body,
        in_specs=[vmem, vmem, hbm, hbm, vmem, vmem, vmem],
        out_specs=hbm,
        out_shape=jax.ShapeDtypeStruct(arrived.shape, jnp.bfloat16),
        scratch_shapes=[
            pltpu.VMEM(later.shape, jnp.bfloat16),
            pltpu.VMEM(spread.shape, jnp.bfloat16),
            pltpu.VMEM((slots, total, 2 * count), jnp.bfloat16),
            pltpu.VMEM((slots, total, 3 * count), jnp.bfloat16),
            pltpu.VMEM((slots, devices, rows, unknowns), jnp.bfloat16),
            pltpu.SemaphoreType.DMA(()),
            pltpu.SemaphoreType.DMA(()),
            pltpu.SemaphoreType.DMA((slots,)),
        ],
        compiler_params=params,
        name="far",
    )(held(arrived), held(gather[:, :, :width]), far_away(later), far_away(spread), *[held(x) for x in (translate, cosine, sine)])


def both_parts(block):
    return jnp.concatenate([block[0], block[1]], 1)


def joined(matrices, vectors):
    angles = vectors[0].shape[1] // 2
    by_re = by_im = 0.0
    for matrix, vector in zip(matrices, vectors):
        by_re += jnp.dot(matrix[0], vector, preferred_element_type=jnp.float32)
        by_im += jnp.dot(matrix[1], vector, preferred_element_type=jnp.float32)
    return by_re[:, :angles] - by_im[:, angles:], by_re[:, angles:] + by_im[:, :angles]


def near_body(place_ref, mask_ref, currents_ref, blocks_ref, out_ref):
    boxes, _, unknowns, angles = currents_ref.shape
    box = pl.program_id(0)
    own = place_ref[0] * boxes + box
    zero = jnp.zeros((unknowns, 2 * angles), jnp.bfloat16)
    here = both_parts(currents_ref[box])
    before = both_parts(currents_ref[jnp.maximum(box - 1, 0)])
    after = both_parts(currents_ref[jnp.minimum(box + 1, boxes - 1)])
    before = jnp.where((mask_ref[0, own] == 1) & (box > 0), before, zero)
    after = jnp.where((mask_ref[1, own] == 1) & (box < boxes - 1), after, zero)
    blocks = blocks_ref[0]
    out_ref[0, 0], out_ref[0, 1] = joined(
        [blocks[0], blocks[1], blocks[2]], [here, before, after]
    )


def near_field(currents, near_blocks, near_mask, place):
    boxes, _, unknowns, angles = currents.shape
    return pl.pallas_call(
        near_body,
        grid_spec=pltpu.PrefetchScalarGridSpec(
            num_scalar_prefetch=2,
            grid=(boxes,),
            in_specs=[
                vmem,
                pl.BlockSpec((1, 3, 2, unknowns, unknowns), lambda i, *_: (i, 0, 0, 0, 0)),
            ],
            out_specs=pl.BlockSpec((1, 2, unknowns, angles), lambda i, *_: (i, 0, 0, 0)),
        ),
        out_shape=pltpu.HBM(currents.shape, jnp.float32),
        compiler_params=params,
        name="near",
    )(place, near_mask, currents, near_blocks)


def rim_body(place_ref, mask_ref, near_ref, one_ref, two_ref, blocks_hbm, out_ref, rim_ref, sems):
    boxes, _, unknowns, angles = near_ref.shape
    even = lax.rem(place_ref[0], 2) == 0
    sides = ((0, 1), (boxes - 1, 2))
    loads = [
        pltpu.make_async_copy(blocks_hbm.at[box, which], rim_ref.at[which - 1], sems.at[which - 1])
        for box, which in sides
    ]
    for load in loads:
        load.start()
    for box in range(1, boxes - 1):
        out_ref[box] = near_ref[box].astype(jnp.bfloat16)
    for load in loads:
        load.wait()
    zero = jnp.zeros((unknowns, 2 * angles), jnp.bfloat16)
    totals = {}
    one, two = both_parts(one_ref[0]), both_parts(two_ref[0])
    edge = {1: jnp.where(even, two, one), 2: jnp.where(even, one, two)}
    for box, which in sides:
        on = mask_ref[which - 1, place_ref[0] * boxes + box] == 1
        vectors = jnp.where(on, edge[which], zero)
        more = joined([rim_ref[which - 1]], [vectors])
        base = totals.get(box, (near_ref[box, 0], near_ref[box, 1]))
        totals[box] = (base[0] + more[0], base[1] + more[1])
    for box, total in totals.items():
        out_ref[box, 0] = total[0].astype(jnp.bfloat16)
        out_ref[box, 1] = total[1].astype(jnp.bfloat16)


def with_rims(near, one, two, near_blocks, near_mask, place):
    unknowns = near.shape[2]
    scalars = pl.BlockSpec(memory_space=pltpu.SMEM)
    return pl.pallas_call(
        rim_body,
        in_specs=[scalars, scalars, vmem, vmem, vmem, hbm],
        out_specs=vmem,
        out_shape=pltpu.VMEM(near.shape, jnp.bfloat16),
        scratch_shapes=[
            pltpu.VMEM((2, 2, unknowns, unknowns), jnp.bfloat16),
            pltpu.SemaphoreType.DMA((2,)),
        ],
        compiler_params=params,
        name="rim",
    )(place, near_mask, near, one, two, far_away(near_blocks))


def edges(currents, place):
    count = lax.axis_size(axes)
    even = lax.rem(place[0], 2) == 0
    first, last = currents[:1], currents[-1:]
    above = [(i, i ^ 1) for i in range(count) if i ^ 1 < count]
    below = [(i, i + 1) for i in range(1, count - 1, 2)]
    below = below + [(target, source) for source, target in below]
    one = lax.ppermute(far_away(jnp.where(even, last, first)), axes, above)
    two = lax.ppermute(far_away(jnp.where(even, first, last)), axes, below)
    return one, two


def routed(values):
    sizes = [lax.axis_size(axis) for axis in axes]
    split = values.reshape(values.shape[:-1] + (*sizes, -1))
    lead = values.ndim - 1
    order = [*range(lead), *(lead + axes.index(axis) for axis in route), lead + len(axes)]
    return split.transpose(order).reshape(values.shape)


def exchange(value):
    return lax.all_to_all(value, route, split_axis=0, concat_axis=0, tiled=True)


def product(currents, near_blocks, near_mask, aggregate, disaggregate, centers):
    devices = lax.axis_size(axes)
    angles_each = currents.shape[3] // devices
    chunks = math.gcd(chunks_wanted, angles_each)
    dir_count = aggregate.shape[1]
    place = lax.axis_index(axes).astype(jnp.int32).reshape(1)

    packed = pack(currents, devices, chunks)
    arrived = [exchange(x) for x in packed]
    one, two = edges(currents, place)
    gather = aggregate.transpose(0, 2, 1)
    turned = disaggregate.transpose(0, 2, 1)
    spread = jnp.concatenate([turned[1], turned[0]], 0)
    names = jnp.arange(centers.shape[1], dtype=jnp.int32)
    points = routed(centers)
    translate = far_matrix(points, routed(near_mask), routed(names))
    theta = phase_angles(points, dir_count)
    cosine = jnp.cos(theta)
    sine = jnp.sin(theta)
    far = [far_field(x, gather, spread, translate, cosine, sine) for x in arrived]
    pieces = [exchange(x) for x in far]
    near = far_away(near_field(currents, near_blocks, near_mask, place))
    near = with_rims(near, one, two, near_blocks, near_mask, place)
    return unpack(near, pieces, devices)


def solution(mesh):
    return jax.shard_map(
        product,
        mesh=mesh,
        in_specs=(
            P(axes, None, None, None),
            P(axes, None, None, None, None),
            P(),
            P(),
            P(),
            P(),
        ),
        out_specs=P(axes, None, None, None),
        check_vma=False,
    )
```

```python
import functools
import math

import jax
import jax.numpy as jnp
from jax import lax
from jax.experimental import pallas as pl
from jax.experimental.pallas import tpu as pltpu
from jax.sharding import PartitionSpec as P


wave_number = 2.0
far_gain = 8.0
golden_turn = 2.399963229728653
axes = ("box", "dir")
route = ("dir", "box")
chunks_wanted = 1
packed = pltpu.CompilerParams(vmem_limit_bytes=20 << 20)
far_rows = 1024
pack_waits = 2
far_slots = 1
hbm = pl.BlockSpec(memory_space=pltpu.HBM)
vmem = pl.BlockSpec(memory_space=pltpu.VMEM)
params = pltpu.CompilerParams(vmem_limit_bytes=20 << 20)


def direction_cosines(count):
    order = jnp.arange(count, dtype=jnp.int32).astype(jnp.float32)
    height = 1.0 - (2.0 * order + 1.0) / count
    radial = jnp.sqrt(1.0 - height * height)
    azimuth = order * golden_turn
    return (radial * jnp.cos(azimuth), radial * jnp.sin(azimuth), height)


def phase_angles(points, count):
    dir_x, dir_y, dir_z = direction_cosines(count)
    return wave_number * (
        points[0][:, None] * dir_x[None, :]
        + points[1][:, None] * dir_y[None, :]
        + points[2][:, None] * dir_z[None, :]
    )


def far_matrix(centers, near_mask, names):
    total_boxes = centers.shape[1]
    squared = jnp.zeros((total_boxes, total_boxes), jnp.float32)
    for axis_number in range(3):
        spread = centers[axis_number][:, None] - centers[axis_number][None, :]
        squared = squared + spread * spread
    spacing = jnp.sqrt(1.0 + squared)
    kernel = jnp.cos(wave_number * spacing) / (1.0 + spacing) * (far_gain / math.sqrt(total_boxes))
    rows = names[:, None]
    cols = names[None, :]
    linked = (
        (cols == rows)
        | (cols == rows - 1) & (near_mask[0][:, None] == 1)
        | (cols == rows + 1) & (near_mask[1][:, None] == 1)
    )
    return jnp.where(linked, 0.0, kernel).astype(jnp.bfloat16)


def swap_matrix(outer, inner):
    size = outer * inner
    row = lax.broadcasted_iota(jnp.int32, (size, size), 0)
    col = lax.broadcasted_iota(jnp.int32, (size, size), 1)
    source = lax.rem(row, inner) * outer + lax.div(row, inner)
    return jnp.where(source == col, 1.0, 0.0).astype(jnp.bfloat16)


def held(value):
    return pltpu.with_memory_space_constraint(value, pltpu.VMEM)


def far_away(value):
    return pltpu.with_memory_space_constraint(value, pltpu.HBM)


def pack_body(currents_ref, *refs, devices, angles_each, group):
    outs, (loaded_ref, turned_ref, mixed_ref, load_sems, store_sems) = refs[:-5], refs[-5:]
    boxes, _, unknowns, angles = currents_ref.shape
    rows = 2 * boxes
    loads = [
        pltpu.make_async_copy(currents_ref.at[box], loaded_ref.at[box], load_sems.at[box])
        for box in range(boxes)
    ]
    for load in loads:
        load.start()
    swap = swap_matrix(group, rows)
    for box in range(boxes):
        if box % pack_waits == 0:
            for load in loads[box : box + pack_waits]:
                load.wait()
        for part in range(2):
            turned_ref[part * boxes + box] = loaded_ref[box, part].T
    per_out = angles_each // len(outs)
    stores = []
    for number, first in enumerate(range(0, angles, group)):
        own, device = divmod(first, devices)
        tile = turned_ref[:, first : first + group, :].reshape(rows * group, unknowns)
        mixed = jnp.dot(swap, tile, preferred_element_type=jnp.float32)
        mixed_ref[number] = mixed.astype(jnp.bfloat16).reshape(group, rows, unknowns)
        which, slot = divmod(own, per_out)
        target = outs[which].at[pl.ds(device, group), slot]
        store = pltpu.make_async_copy(mixed_ref.at[number], target, store_sems.at[number])
        store.start()
        stores.append(store)
    for store in stores:
        store.wait()


def pack(currents, devices, chunks):
    boxes, _, unknowns, angles = currents.shape
    angles_each = angles // devices
    group = math.gcd(16, devices)
    rows = 2 * boxes
    body = functools.partial(pack_body, devices=devices, angles_each=angles_each, group=group)
    shape = jax.ShapeDtypeStruct((devices, angles_each // chunks, rows, unknowns), jnp.bfloat16)
    return pl.pallas_call(
        body,
        in_specs=[hbm],
        out_specs=[hbm] * chunks,
        out_shape=[shape] * chunks,
        scratch_shapes=[
            pltpu.VMEM(currents.shape, jnp.bfloat16),
            pltpu.VMEM((rows, angles, unknowns), jnp.bfloat16),
            pltpu.VMEM((angles // group, group, rows, unknowns), jnp.bfloat16),
            pltpu.SemaphoreType.DMA((boxes,)),
            pltpu.SemaphoreType.DMA((angles // group,)),
        ],
        compiler_params=params,
        name="pack",
    )(far_away(currents))


def unpack_body(near_ref, *refs, devices, angles_each, group):
    ins, (out_ref, turned_ref, done_ref, sems) = refs[:-4], refs[-4:]
    boxes, _, unknowns, angles = near_ref.shape
    rows = 2 * boxes
    per_in = angles_each // len(ins)
    swap = swap_matrix(rows, group)
    for first in range(0, angles, group):
        own, device = divmod(first, devices)
        which, slot = divmod(own, per_in)
        tile = ins[which][device : device + group, slot].reshape(rows * group, unknowns)
        mixed = jnp.dot(swap, tile, preferred_element_type=jnp.float32)
        turned_ref[:, first : first + group, :] = mixed.astype(jnp.bfloat16).reshape(
            rows, group, unknowns
        )
    stores = [
        pltpu.make_async_copy(done_ref.at[box], out_ref.at[box], sems.at[box])
        for box in range(boxes)
    ]
    for box, store in enumerate(stores):
        for part in range(2):
            far = turned_ref[part * boxes + box].T.astype(jnp.float32)
            near = near_ref[box, part].astype(jnp.float32)
            done_ref[box, part] = (near + far).astype(jnp.bfloat16)
        store.start()
    for store in stores:
        store.wait()


def unpack(near, pieces, devices):
    boxes, _, unknowns, angles = near.shape
    angles_each = angles // devices
    group = math.gcd(16, devices)
    rows = 2 * boxes
    body = functools.partial(unpack_body, devices=devices, angles_each=angles_each, group=group)
    return pl.pallas_call(
        body,
        in_specs=[vmem] * (1 + len(pieces)),
        out_specs=hbm,
        out_shape=jax.ShapeDtypeStruct(near.shape, jnp.bfloat16),
        scratch_shapes=[
            pltpu.VMEM((rows, angles, unknowns), jnp.bfloat16),
            pltpu.VMEM(near.shape, jnp.bfloat16),
            pltpu.SemaphoreType.DMA((boxes,)),
        ],
        compiler_params=packed,
        name="unpack",
    )(held(near), *[held(x) for x in pieces])


def far_body(
    arrived_ref, gather_ref, gather_hbm, spread_hbm, translate_ref, cos_ref, sin_ref, out_ref,
    later_ref, spread_ref, pat_ref, rec_ref, done_ref, later_sem, load_sem, sems,
):
    devices, slots, rows, unknowns = arrived_ref.shape
    boxes = rows // 2
    total, count = cos_ref.shape
    width = gather_ref.shape[2]
    later = pltpu.make_async_copy(gather_hbm, later_ref, later_sem)
    later.start()
    load = pltpu.make_async_copy(spread_hbm, spread_ref, load_sem)
    load.start()
    some = math.gcd(devices, max(1, far_rows // (slots * rows)))

    def product(left, right):
        return jnp.dot(left, right, preferred_element_type=jnp.float32)

    for low in range(0, count, width):
        high = low + width
        table_ref = later_ref if low else gather_ref
        start = max(0, low - width)
        if low == width:
            later.wait()
        for first in range(0, devices, some):
            arrived = arrived_ref[first : first + some].reshape(some * slots * rows, unknowns)
            span = slice(first * boxes, (first + some) * boxes)
            shape = (some, slots, 2, boxes, width)
            by_re = product(arrived, table_ref[0, :, start : start + width]).reshape(shape)
            by_im = product(arrived, table_ref[1, :, start : start + width]).reshape(shape)
            cosine = cos_ref[span, low:high].reshape(some, boxes, width)
            sine = sin_ref[span, low:high].reshape(some, boxes, width)
            for slot in range(slots):
                pat_re = by_re[:, slot, 0] - by_im[:, slot, 1]
                pat_im = by_re[:, slot, 1] + by_im[:, slot, 0]
                out_re = (cosine * pat_re + sine * pat_im).reshape(some * boxes, width)
                out_im = (cosine * pat_im - sine * pat_re).reshape(some * boxes, width)
                pat_ref[slot, span, low:high] = out_re.astype(jnp.bfloat16)
                pat_ref[slot, span, count + low : count + high] = out_im.astype(jnp.bfloat16)
    load.wait()
    stores = []
    pairs = math.gcd(slots, far_slots)
    for begin in range(0, slots, pairs):
        for slot in range(begin, begin + pairs):
            for low in range(0, count, width):
                high = low + width
                translate = translate_ref[...]
                sum_re = product(translate, pat_ref[slot, :, low:high])
                sum_im = product(translate, pat_ref[slot, :, count + low : count + high])
                cosine = cos_ref[:, low:high]
                sine = sin_ref[:, low:high]
                rec_re = (cosine * sum_re - sine * sum_im).astype(jnp.bfloat16)
                rec_im = (cosine * sum_im + sine * sum_re).astype(jnp.bfloat16)
                rec_ref[slot, :, low:high] = rec_re
                rec_ref[slot, :, count + low : count + high] = rec_im
                rec_ref[slot, :, 2 * count + low : 2 * count + high] = -rec_re
        many = pairs * total
        whole = (pairs, devices, 1, boxes, unknowns)
        rec_re_im = rec_ref[begin : begin + pairs, :, : 2 * count].reshape(many, 2 * count)
        rec_im_re = rec_ref[begin : begin + pairs, :, count:].reshape(many, 2 * count)
        imag = product(rec_re_im, spread_ref[...]).reshape(whole)
        real = product(rec_im_re, spread_ref[...]).reshape(whole)
        both = jnp.concatenate([-real, imag], 2).reshape(pairs, devices, rows, unknowns)
        done_ref[begin : begin + pairs] = both.astype(jnp.bfloat16)
        for slot in range(begin, begin + pairs):
            store = pltpu.make_async_copy(done_ref.at[slot], out_ref.at[:, slot], sems.at[slot])
            store.start()
            stores.append(store)
    for store in stores:
        store.wait()


def far_field(arrived, gather, spread, translate, cosine, sine):
    devices, slots, rows, unknowns = arrived.shape
    total, count = cosine.shape
    width = math.gcd(count // 2, 256)
    later = gather[:, :, width:]
    return pl.pallas_call(
        far_body,
        in_specs=[vmem, vmem, hbm, hbm, vmem, vmem, vmem],
        out_specs=hbm,
        out_shape=jax.ShapeDtypeStruct(arrived.shape, jnp.bfloat16),
        scratch_shapes=[
            pltpu.VMEM(later.shape, jnp.bfloat16),
            pltpu.VMEM(spread.shape, jnp.bfloat16),
            pltpu.VMEM((slots, total, 2 * count), jnp.bfloat16),
            pltpu.VMEM((slots, total, 3 * count), jnp.bfloat16),
            pltpu.VMEM((slots, devices, rows, unknowns), jnp.bfloat16),
            pltpu.SemaphoreType.DMA(()),
            pltpu.SemaphoreType.DMA(()),
            pltpu.SemaphoreType.DMA((slots,)),
        ],
        compiler_params=params,
        name="far",
    )(held(arrived), held(gather[:, :, :width]), far_away(later), far_away(spread), *[held(x) for x in (translate, cosine, sine)])


def both_parts(block):
    return jnp.concatenate([block[0], block[1]], 1)


def joined(matrices, vectors):
    angles = vectors[0].shape[1] // 2
    by_re = by_im = 0.0
    for matrix, vector in zip(matrices, vectors):
        by_re += jnp.dot(matrix[0], vector, preferred_element_type=jnp.float32)
        by_im += jnp.dot(matrix[1], vector, preferred_element_type=jnp.float32)
    return by_re[:, :angles] - by_im[:, angles:], by_re[:, angles:] + by_im[:, :angles]


def near_body(place_ref, mask_ref, currents_ref, blocks_ref, out_ref):
    boxes, _, unknowns, angles = currents_ref.shape
    box = pl.program_id(0)
    own = place_ref[0] * boxes + box
    zero = jnp.zeros((unknowns, 2 * angles), jnp.bfloat16)
    here = both_parts(currents_ref[box])
    before = both_parts(currents_ref[jnp.maximum(box - 1, 0)])
    after = both_parts(currents_ref[jnp.minimum(box + 1, boxes - 1)])
    before = jnp.where((mask_ref[0, own] == 1) & (box > 0), before, zero)
    after = jnp.where((mask_ref[1, own] == 1) & (box < boxes - 1), after, zero)
    blocks = blocks_ref[0]
    out_ref[0, 0], out_ref[0, 1] = joined(
        [blocks[0], blocks[1], blocks[2]], [here, before, after]
    )


def near_field(currents, near_blocks, near_mask, place):
    boxes, _, unknowns, angles = currents.shape
    return pl.pallas_call(
        near_body,
        grid_spec=pltpu.PrefetchScalarGridSpec(
            num_scalar_prefetch=2,
            grid=(boxes,),
            in_specs=[
                vmem,
                pl.BlockSpec((1, 3, 2, unknowns, unknowns), lambda i, *_: (i, 0, 0, 0, 0)),
            ],
            out_specs=pl.BlockSpec((1, 2, unknowns, angles), lambda i, *_: (i, 0, 0, 0)),
        ),
        out_shape=pltpu.HBM(currents.shape, jnp.float32),
        compiler_params=params,
        name="near",
    )(place, near_mask, currents, near_blocks)


def rim_body(place_ref, mask_ref, near_ref, one_ref, two_ref, blocks_hbm, out_ref, rim_ref, sems):
    boxes, _, unknowns, angles = near_ref.shape
    even = lax.rem(place_ref[0], 2) == 0
    sides = ((0, 1), (boxes - 1, 2))
    loads = [
        pltpu.make_async_copy(blocks_hbm.at[box, which], rim_ref.at[which - 1], sems.at[which - 1])
        for box, which in sides
    ]
    for load in loads:
        load.start()
    for box in range(1, boxes - 1):
        out_ref[box] = near_ref[box].astype(jnp.bfloat16)
    for load in loads:
        load.wait()
    zero = jnp.zeros((unknowns, 2 * angles), jnp.bfloat16)
    totals = {}
    one, two = both_parts(one_ref[0]), both_parts(two_ref[0])
    edge = {1: jnp.where(even, two, one), 2: jnp.where(even, one, two)}
    for box, which in sides:
        on = mask_ref[which - 1, place_ref[0] * boxes + box] == 1
        vectors = jnp.where(on, edge[which], zero)
        more = joined([rim_ref[which - 1]], [vectors])
        base = totals.get(box, (near_ref[box, 0], near_ref[box, 1]))
        totals[box] = (base[0] + more[0], base[1] + more[1])
    for box, total in totals.items():
        out_ref[box, 0] = total[0].astype(jnp.bfloat16)
        out_ref[box, 1] = total[1].astype(jnp.bfloat16)


def with_rims(near, one, two, near_blocks, near_mask, place):
    unknowns = near.shape[2]
    scalars = pl.BlockSpec(memory_space=pltpu.SMEM)
    return pl.pallas_call(
        rim_body,
        in_specs=[scalars, scalars, vmem, vmem, vmem, hbm],
        out_specs=vmem,
        out_shape=pltpu.VMEM(near.shape, jnp.bfloat16),
        scratch_shapes=[
            pltpu.VMEM((2, 2, unknowns, unknowns), jnp.bfloat16),
            pltpu.SemaphoreType.DMA((2,)),
        ],
        compiler_params=params,
        name="rim",
    )(place, near_mask, near, one, two, far_away(near_blocks))


def edges(currents, place):
    count = lax.axis_size(axes)
    even = lax.rem(place[0], 2) == 0
    first, last = currents[:1], currents[-1:]
    above = [(i, i ^ 1) for i in range(count) if i ^ 1 < count]
    below = [(i, i + 1) for i in range(1, count - 1, 2)]
    below = below + [(target, source) for source, target in below]
    one = lax.ppermute(far_away(jnp.where(even, last, first)), axes, above)
    two = lax.ppermute(far_away(jnp.where(even, first, last)), axes, below)
    return one, two


def routed(values):
    sizes = [lax.axis_size(axis) for axis in axes]
    split = values.reshape(values.shape[:-1] + (*sizes, -1))
    lead = values.ndim - 1
    order = [*range(lead), *(lead + axes.index(axis) for axis in route), lead + len(axes)]
    return split.transpose(order).reshape(values.shape)


def exchange(value):
    return lax.all_to_all(value, route, split_axis=0, concat_axis=0, tiled=True)


def product(currents, near_blocks, near_mask, aggregate, disaggregate, centers):
    devices = lax.axis_size(axes)
    angles_each = currents.shape[3] // devices
    chunks = math.gcd(chunks_wanted, angles_each)
    dir_count = aggregate.shape[1]
    place = lax.axis_index(axes).astype(jnp.int32).reshape(1)

    packed = pack(currents, devices, chunks)
    arrived = [exchange(x) for x in packed]
    one, two = edges(currents, place)
    gather = aggregate.transpose(0, 2, 1)
    turned = disaggregate.transpose(0, 2, 1)
    spread = jnp.concatenate([turned[1], turned[0]], 0)
    names = jnp.arange(centers.shape[1], dtype=jnp.int32)
    points = routed(centers)
    translate = far_matrix(points, routed(near_mask), routed(names))
    theta = phase_angles(points, dir_count)
    cosine = jnp.cos(theta)
    sine = jnp.sin(theta)
    far = [far_field(x, gather, spread, translate, cosine, sine) for x in arrived]
    pieces = [exchange(x) for x in far]
    near = far_away(near_field(currents, near_blocks, near_mask, place))
    near = with_rims(near, one, two, near_blocks, near_mask, place)
    return unpack(near, pieces, devices)


def solution(mesh):
    return jax.shard_map(
        product,
        mesh=mesh,
        in_specs=(
            P(axes, None, None, None),
            P(axes, None, None, None, None),
            P(),
            P(),
            P(),
            P(),
        ),
        out_specs=P(axes, None, None, None),
        check_vma=False,
    )
```

```python
import functools
import math

import jax
import jax.numpy as jnp
import numpy as np
from jax import lax
from jax.experimental import pallas as pl
from jax.experimental.pallas import tpu as pltpu
from jax.sharding import PartitionSpec as P


wave_number = 2.0
far_gain = 8.0
golden_turn = 2.399963229728653
axes = ("box", "dir")
route = ("dir", "box")
chunks_wanted = 1
packed = pltpu.CompilerParams(vmem_limit_bytes=20 << 20)
far_rows = 1024
pack_waits = 4
far_slots = 1
hbm = pl.BlockSpec(memory_space=pltpu.HBM)
vmem = pl.BlockSpec(memory_space=pltpu.VMEM)
params = pltpu.CompilerParams(vmem_limit_bytes=20 << 20)


def direction_cosines(count):
    order = jnp.arange(count, dtype=jnp.int32).astype(jnp.float32)
    height = 1.0 - (2.0 * order + 1.0) / count
    radial = jnp.sqrt(1.0 - height * height)
    azimuth = order * golden_turn
    return (radial * jnp.cos(azimuth), radial * jnp.sin(azimuth), height)


def phase_angles(points, count):
    dir_x, dir_y, dir_z = direction_cosines(count)
    return wave_number * (
        points[0][:, None] * dir_x[None, :]
        + points[1][:, None] * dir_y[None, :]
        + points[2][:, None] * dir_z[None, :]
    )


def far_matrix(centers, near_mask, names):
    total_boxes = centers.shape[1]
    squared = jnp.zeros((total_boxes, total_boxes), jnp.float32)
    for axis_number in range(3):
        spread = centers[axis_number][:, None] - centers[axis_number][None, :]
        squared = squared + spread * spread
    spacing = jnp.sqrt(1.0 + squared)
    kernel = jnp.cos(wave_number * spacing) / (1.0 + spacing) * (far_gain / math.sqrt(total_boxes))
    rows = names[:, None]
    cols = names[None, :]
    linked = (
        (cols == rows)
        | (cols == rows - 1) & (near_mask[0][:, None] == 1)
        | (cols == rows + 1) & (near_mask[1][:, None] == 1)
    )
    return jnp.where(linked, 0.0, kernel).astype(jnp.bfloat16)


def swap_matrix(outer, inner):
    size = outer * inner
    row = lax.broadcasted_iota(jnp.int32, (size, size), 0)
    col = lax.broadcasted_iota(jnp.int32, (size, size), 1)
    source = lax.rem(row, inner) * outer + lax.div(row, inner)
    return jnp.where(source == col, 1.0, 0.0).astype(jnp.bfloat16)


def swap_table(outer, inner):
    row = np.arange(outer * inner)
    source = (row % inner) * outer + row // inner
    return jnp.asarray(source[:, None] == row[None, :], jnp.bfloat16)


def held(value):
    return pltpu.with_memory_space_constraint(value, pltpu.VMEM)


def far_away(value):
    return pltpu.with_memory_space_constraint(value, pltpu.HBM)


def pack_body(currents_ref, *refs, devices, angles_each, group):
    outs, (loaded_ref, turned_ref, mixed_ref, load_sems, store_sems) = refs[:-5], refs[-5:]
    boxes, _, unknowns, angles = currents_ref.shape
    rows = 2 * boxes
    loads = [
        pltpu.make_async_copy(currents_ref.at[box], loaded_ref.at[box], load_sems.at[box])
        for box in range(boxes)
    ]
    for load in loads:
        load.start()
    swap = swap_matrix(group, rows)
    for box in range(boxes):
        if box % pack_waits == 0:
            for load in loads[box : box + pack_waits]:
                load.wait()
        for part in range(2):
            turned_ref[part * boxes + box] = loaded_ref[box, part].T
    per_out = angles_each // len(outs)
    stores = []
    for number, first in enumerate(range(0, angles, group)):
        own, device = divmod(first, devices)
        tile = turned_ref[:, first : first + group, :].reshape(rows * group, unknowns)
        mixed = jnp.dot(swap, tile, preferred_element_type=jnp.float32)
        mixed_ref[number] = mixed.astype(jnp.bfloat16).reshape(group, rows, unknowns)
        which, slot = divmod(own, per_out)
        target = outs[which].at[pl.ds(device, group), slot]
        store = pltpu.make_async_copy(mixed_ref.at[number], target, store_sems.at[number])
        store.start()
        stores.append(store)
    for store in stores:
        store.wait()


def pack(currents, devices, chunks):
    boxes, _, unknowns, angles = currents.shape
    angles_each = angles // devices
    group = math.gcd(16, devices)
    rows = 2 * boxes
    body = functools.partial(pack_body, devices=devices, angles_each=angles_each, group=group)
    shape = jax.ShapeDtypeStruct((devices, angles_each // chunks, rows, unknowns), jnp.bfloat16)
    return pl.pallas_call(
        body,
        in_specs=[hbm],
        out_specs=[hbm] * chunks,
        out_shape=[shape] * chunks,
        scratch_shapes=[
            pltpu.VMEM(currents.shape, jnp.bfloat16),
            pltpu.VMEM((rows, angles, unknowns), jnp.bfloat16),
            pltpu.VMEM((angles // group, group, rows, unknowns), jnp.bfloat16),
            pltpu.SemaphoreType.DMA((boxes,)),
            pltpu.SemaphoreType.DMA((angles // group,)),
        ],
        compiler_params=params,
        name="pack",
    )(far_away(currents))


def unpack_body(near_ref, swap_ref, *refs, devices, angles_each, group):
    ins, (out_ref, turned_ref, done_ref, sems) = refs[:-4], refs[-4:]
    boxes, _, unknowns, angles = near_ref.shape
    rows = 2 * boxes
    per_in = angles_each // len(ins)
    swap = swap_ref[...]
    for first in range(0, angles, group):
        own, device = divmod(first, devices)
        which, slot = divmod(own, per_in)
        tile = ins[which][device : device + group, slot].reshape(rows * group, unknowns)
        mixed = jnp.dot(swap, tile, preferred_element_type=jnp.float32)
        turned_ref[:, first : first + group, :] = mixed.astype(jnp.bfloat16).reshape(
            rows, group, unknowns
        )
    stores = [
        pltpu.make_async_copy(done_ref.at[box], out_ref.at[box], sems.at[box])
        for box in range(boxes)
    ]
    for box, store in enumerate(stores):
        for part in range(2):
            far = turned_ref[part * boxes + box].T.astype(jnp.float32)
            near = near_ref[box, part].astype(jnp.float32)
            done_ref[box, part] = (near + far).astype(jnp.bfloat16)
        store.start()
    for store in stores:
        store.wait()


def unpack(near, pieces, devices):
    boxes, _, unknowns, angles = near.shape
    angles_each = angles // devices
    group = math.gcd(16, devices)
    rows = 2 * boxes
    body = functools.partial(unpack_body, devices=devices, angles_each=angles_each, group=group)
    return pl.pallas_call(
        body,
        in_specs=[vmem] * (2 + len(pieces)),
        out_specs=hbm,
        out_shape=jax.ShapeDtypeStruct(near.shape, jnp.bfloat16),
        scratch_shapes=[
            pltpu.VMEM((rows, angles, unknowns), jnp.bfloat16),
            pltpu.VMEM(near.shape, jnp.bfloat16),
            pltpu.SemaphoreType.DMA((boxes,)),
        ],
        compiler_params=packed,
        name="unpack",
    )(held(near), held(swap_table(rows, group)), *[held(x) for x in pieces])


def far_body(
    arrived_ref, gather_ref, gather_hbm, spread_hbm, translate_ref, cos_ref, sin_ref, out_ref,
    later_ref, spread_ref, pat_ref, rec_ref, done_ref, later_sem, load_sem, sems,
):
    devices, slots, rows, unknowns = arrived_ref.shape
    boxes = rows // 2
    total, count = cos_ref.shape
    width = gather_ref.shape[2]
    later = pltpu.make_async_copy(gather_hbm, later_ref, later_sem)
    later.start()
    load = pltpu.make_async_copy(spread_hbm, spread_ref, load_sem)
    load.start()
    some = math.gcd(devices, max(1, far_rows // (slots * rows)))

    def product(left, right):
        return jnp.dot(left, right, preferred_element_type=jnp.float32)

    for low in range(0, count, width):
        high = low + width
        table_ref = later_ref if low else gather_ref
        start = max(0, low - width)
        if low == width:
            later.wait()
        for first in range(0, devices, some):
            arrived = arrived_ref[first : first + some].reshape(some * slots * rows, unknowns)
            span = slice(first * boxes, (first + some) * boxes)
            shape = (some, slots, 2, boxes, width)
            by_re = product(arrived, table_ref[0, :, start : start + width]).reshape(shape)
            by_im = product(arrived, table_ref[1, :, start : start + width]).reshape(shape)
            cosine = cos_ref[span, low:high].reshape(some, boxes, width)
            sine = sin_ref[span, low:high].reshape(some, boxes, width)
            for slot in range(slots):
                pat_re = by_re[:, slot, 0] - by_im[:, slot, 1]
                pat_im = by_re[:, slot, 1] + by_im[:, slot, 0]
                out_re = (cosine * pat_re + sine * pat_im).reshape(some * boxes, width)
                out_im = (cosine * pat_im - sine * pat_re).reshape(some * boxes, width)
                pat_ref[slot, span, low:high] = out_re.astype(jnp.bfloat16)
                pat_ref[slot, span, count + low : count + high] = out_im.astype(jnp.bfloat16)
    load.wait()
    stores = []
    pairs = math.gcd(slots, far_slots)
    for begin in range(0, slots, pairs):
        for slot in range(begin, begin + pairs):
            for low in range(0, count, width):
                high = low + width
                translate = translate_ref[...]
                sum_re = product(translate, pat_ref[slot, :, low:high])
                sum_im = product(translate, pat_ref[slot, :, count + low : count + high])
                cosine = cos_ref[:, low:high]
                sine = sin_ref[:, low:high]
                rec_re = (cosine * sum_re - sine * sum_im).astype(jnp.bfloat16)
                rec_im = (cosine * sum_im + sine * sum_re).astype(jnp.bfloat16)
                rec_ref[slot, :, low:high] = rec_re
                rec_ref[slot, :, count + low : count + high] = rec_im
                rec_ref[slot, :, 2 * count + low : 2 * count + high] = -rec_re
        many = pairs * total
        whole = (pairs, devices, 1, boxes, unknowns)
        rec_re_im = rec_ref[begin : begin + pairs, :, : 2 * count].reshape(many, 2 * count)
        rec_im_re = rec_ref[begin : begin + pairs, :, count:].reshape(many, 2 * count)
        imag = product(rec_re_im, spread_ref[...]).reshape(whole)
        real = product(rec_im_re, spread_ref[...]).reshape(whole)
        both = jnp.concatenate([-real, imag], 2).reshape(pairs, devices, rows, unknowns)
        done_ref[begin : begin + pairs] = both.astype(jnp.bfloat16)
        for slot in range(begin, begin + pairs):
            store = pltpu.make_async_copy(done_ref.at[slot], out_ref.at[:, slot], sems.at[slot])
            store.start()
            stores.append(store)
    for store in stores:
        store.wait()


def far_field(arrived, gather, spread, translate, cosine, sine):
    devices, slots, rows, unknowns = arrived.shape
    total, count = cosine.shape
    width = math.gcd(count // 2, 256)
    later = gather[:, :, width:]
    return pl.pallas_call(
        far_body,
        in_specs=[vmem, vmem, hbm, hbm, vmem, vmem, vmem],
        out_specs=hbm,
        out_shape=jax.ShapeDtypeStruct(arrived.shape, jnp.bfloat16),
        scratch_shapes=[
            pltpu.VMEM(later.shape, jnp.bfloat16),
            pltpu.VMEM(spread.shape, jnp.bfloat16),
            pltpu.VMEM((slots, total, 2 * count), jnp.bfloat16),
            pltpu.VMEM((slots, total, 3 * count), jnp.bfloat16),
            pltpu.VMEM((slots, devices, rows, unknowns), jnp.bfloat16),
            pltpu.SemaphoreType.DMA(()),
            pltpu.SemaphoreType.DMA(()),
            pltpu.SemaphoreType.DMA((slots,)),
        ],
        compiler_params=params,
        name="far",
    )(held(arrived), held(gather[:, :, :width]), far_away(later), far_away(spread), *[held(x) for x in (translate, cosine, sine)])


def both_parts(block):
    return jnp.concatenate([block[0], block[1]], 1)


def joined(matrices, vectors):
    angles = vectors[0].shape[1] // 2
    by_re = by_im = 0.0
    for matrix, vector in zip(matrices, vectors):
        by_re += jnp.dot(matrix[0], vector, preferred_element_type=jnp.float32)
        by_im += jnp.dot(matrix[1], vector, preferred_element_type=jnp.float32)
    return by_re[:, :angles] - by_im[:, angles:], by_re[:, angles:] + by_im[:, :angles]


def near_body(place_ref, mask_ref, currents_ref, blocks_ref, out_ref):
    boxes, _, unknowns, angles = currents_ref.shape
    box = pl.program_id(0)
    own = place_ref[0] * boxes + box
    zero = jnp.zeros((unknowns, 2 * angles), jnp.bfloat16)
    here = both_parts(currents_ref[box])
    before = both_parts(currents_ref[jnp.maximum(box - 1, 0)])
    after = both_parts(currents_ref[jnp.minimum(box + 1, boxes - 1)])
    before = jnp.where((mask_ref[0, own] == 1) & (box > 0), before, zero)
    after = jnp.where((mask_ref[1, own] == 1) & (box < boxes - 1), after, zero)
    blocks = blocks_ref[0]
    out_ref[0, 0], out_ref[0, 1] = joined(
        [blocks[0], blocks[1], blocks[2]], [here, before, after]
    )


def near_field(currents, near_blocks, near_mask, place):
    boxes, _, unknowns, angles = currents.shape
    return pl.pallas_call(
        near_body,
        grid_spec=pltpu.PrefetchScalarGridSpec(
            num_scalar_prefetch=2,
            grid=(boxes,),
            in_specs=[
                vmem,
                pl.BlockSpec((1, 3, 2, unknowns, unknowns), lambda i, *_: (i, 0, 0, 0, 0)),
            ],
            out_specs=pl.BlockSpec((1, 2, unknowns, angles), lambda i, *_: (i, 0, 0, 0)),
        ),
        out_shape=pltpu.HBM(currents.shape, jnp.float32),
        compiler_params=params,
        name="near",
    )(place, near_mask, currents, near_blocks)


def rim_body(place_ref, mask_ref, near_ref, one_ref, two_ref, blocks_hbm, out_ref, rim_ref, sems):
    boxes, _, unknowns, angles = near_ref.shape
    even = lax.rem(place_ref[0], 2) == 0
    sides = ((0, 1), (boxes - 1, 2))
    loads = [
        pltpu.make_async_copy(blocks_hbm.at[box, which], rim_ref.at[which - 1], sems.at[which - 1])
        for box, which in sides
    ]
    for load in loads:
        load.start()
    for box in range(1, boxes - 1):
        out_ref[box] = near_ref[box].astype(jnp.bfloat16)
    for load in loads:
        load.wait()
    zero = jnp.zeros((unknowns, 2 * angles), jnp.bfloat16)
    totals = {}
    one, two = both_parts(one_ref[0]), both_parts(two_ref[0])
    edge = {1: jnp.where(even, two, one), 2: jnp.where(even, one, two)}
    for box, which in sides:
        on = mask_ref[which - 1, place_ref[0] * boxes + box] == 1
        vectors = jnp.where(on, edge[which], zero)
        more = joined([rim_ref[which - 1]], [vectors])
        base = totals.get(box, (near_ref[box, 0], near_ref[box, 1]))
        totals[box] = (base[0] + more[0], base[1] + more[1])
    for box, total in totals.items():
        out_ref[box, 0] = total[0].astype(jnp.bfloat16)
        out_ref[box, 1] = total[1].astype(jnp.bfloat16)


def with_rims(near, one, two, near_blocks, near_mask, place):
    unknowns = near.shape[2]
    scalars = pl.BlockSpec(memory_space=pltpu.SMEM)
    return pl.pallas_call(
        rim_body,
        in_specs=[scalars, scalars, vmem, vmem, vmem, hbm],
        out_specs=vmem,
        out_shape=pltpu.VMEM(near.shape, jnp.bfloat16),
        scratch_shapes=[
            pltpu.VMEM((2, 2, unknowns, unknowns), jnp.bfloat16),
            pltpu.SemaphoreType.DMA((2,)),
        ],
        compiler_params=params,
        name="rim",
    )(place, near_mask, near, one, two, far_away(near_blocks))


def edges(currents, place):
    count = lax.axis_size(axes)
    even = lax.rem(place[0], 2) == 0
    first, last = currents[:1], currents[-1:]
    above = [(i, i ^ 1) for i in range(count) if i ^ 1 < count]
    below = [(i, i + 1) for i in range(1, count - 1, 2)]
    below = below + [(target, source) for source, target in below]
    one = lax.ppermute(far_away(jnp.where(even, last, first)), axes, above)
    two = lax.ppermute(far_away(jnp.where(even, first, last)), axes, below)
    return one, two


def routed(values):
    sizes = [lax.axis_size(axis) for axis in axes]
    split = values.reshape(values.shape[:-1] + (*sizes, -1))
    lead = values.ndim - 1
    order = [*range(lead), *(lead + axes.index(axis) for axis in route), lead + len(axes)]
    return split.transpose(order).reshape(values.shape)


def exchange(value):
    return lax.all_to_all(value, route, split_axis=0, concat_axis=0, tiled=True)


def product(currents, near_blocks, near_mask, aggregate, disaggregate, centers):
    devices = lax.axis_size(axes)
    angles_each = currents.shape[3] // devices
    chunks = math.gcd(chunks_wanted, angles_each)
    dir_count = aggregate.shape[1]
    place = lax.axis_index(axes).astype(jnp.int32).reshape(1)

    packed = pack(currents, devices, chunks)
    arrived = [exchange(x) for x in packed]
    one, two = edges(currents, place)
    gather = aggregate.transpose(0, 2, 1)
    turned = disaggregate.transpose(0, 2, 1)
    spread = jnp.concatenate([turned[1], turned[0]], 0)
    names = jnp.arange(centers.shape[1], dtype=jnp.int32)
    points = routed(centers)
    translate = far_matrix(points, routed(near_mask), routed(names))
    theta = phase_angles(points, dir_count)
    cosine = jnp.cos(theta)
    sine = jnp.sin(theta)
    far = [far_field(x, gather, spread, translate, cosine, sine) for x in arrived]
    pieces = [exchange(x) for x in far]
    near = far_away(near_field(currents, near_blocks, near_mask, place))
    near = with_rims(near, one, two, near_blocks, near_mask, place)
    return unpack(near, pieces, devices)


def solution(mesh):
    return jax.shard_map(
        product,
        mesh=mesh,
        in_specs=(
            P(axes, None, None, None),
            P(axes, None, None, None, None),
            P(),
            P(),
            P(),
            P(),
        ),
        out_specs=P(axes, None, None, None),
        check_vma=False,
    )
```
